128 devices in a mesh: seg: 32 (over y, z, core), rep: 4 (over x).
Axes of the slice: x: 4, y: 4, z: 4, core: 2. Of those that a mesh axis runs over, the one named last changes fastest.
Arguments:
- speeds: float32 [384, 16384], P(('rep', 'seg')), may hold values from -6 to 6
- w_start: float32 [32], replicated, may hold values from -4 to 4
- b_start: float32 [32], replicated, may hold values from -3 to 3
- w_filter: bfloat16 [2, 32, 32], replicated, may hold values from -0.75 to 0.75
- b_filter: float32 [32], replicated, may hold values from -3 to 3
- w_gate: bfloat16 [2, 32, 32], replicated, may hold values from -0.75 to 0.75
- b_gate: float32 [32], replicated, may hold values from -3 to 3
- adj_cols: int32 [128, 3], P('seg'), may hold values from 0 to 127, as said below
- adj_vals: bfloat16 [128, 3, 128, 128], P('seg'), may hold values from -0.3125 to 0.3125
- w_mix: bfloat16 [32, 96], replicated, may hold values from -0.625 to 0.625
- b_mix: float32 [32], replicated, may hold values from -3 to 3
- w_skip: bfloat16 [256, 32], replicated, may hold values from -1 to 1
- b_skip: float32 [256], replicated, may hold values from -3 to 3
- grad_res: bfloat16 [8, 32, 32, 16384], P('rep', None, None, 'seg'), may hold values from -6 to 6
- grad_skip: bfloat16 [8, 256, 16384], P('rep', None, 'seg'), may hold values from -6 to 6
Outputs:
- res_out: bfloat16 [8, 32, 32, 16384], P('rep', None, None, 'seg')
- skip_out: bfloat16 [8, 256, 16384], P('rep', None, 'seg')
- start_weight_gradient: float32 [32], replicated
- d_start_b: float32 [32], replicated
- d_filter: float32 [2, 32, 32], replicated
- d_filter_b: float32 [32], replicated
- d_gate: float32 [2, 32, 32], replicated
- d_gate_b: float32 [32], replicated
- d_mix: float32 [32, 96], replicated
- d_mix_b: float32 [32], replicated
- d_skip: float32 [256, 32], replicated
- d_skip_b: float32 [256], replicated
The draws below stay inside these ranges and needn't reach their ends.
Inputs may be any that keep to these rules, and one draw needn't show every extreme that they name: adj_cols[i, 0] = i; the 3 entries of a row are distinct and lie within 2 tiles of i; adj_cols[i, 1] is i - 2 or i + 2.
All inputs are finite; a program needn't handle non-finite values.
Results may differ from the reference program's by a relative error of at most 0.01.
Values may be sent and summed in bfloat16 or wider, within the bound.
No kernel may reach another device: no remote copies, remote signals or barrier semaphores. Data moves between devices by JAX's collectives and lax.ppermute only.
A program may use at most 192 MiB of HBM per device.

```python
import math
import jax
import jax.numpy as jnp
from jax import lax

C = 32
SKIP = 256
TILE = 128
K = 3
R = 2
DILATION_SIZE = 16
OUTPUT_STEPS = 32
T_IN = 48
BATCH = 8
NTILES = 128
NSEG = 16384
SNAPS = 384


def draw_adj_cols(key, part):
    tiles = jnp.arange(NTILES, dtype=jnp.int32)
    sign_key, pick_key = jax.random.split(key)
    signs = 2 * jax.random.randint(sign_key, (NTILES,), 0, 2).astype(jnp.int32) - 1
    reached = tiles + signs * R
    outside = (reached < 0) | (reached >= NTILES)
    signs = jnp.where(outside, -signs, signs)
    ones_col = jnp.ones_like(signs)
    candidates = jnp.stack([-ones_col, ones_col, -signs * R], axis=1)
    landing = tiles[:, None] + candidates
    usable = (landing >= 0) & (landing < NTILES)
    scores = jax.random.randint(pick_key, (NTILES, 3), 0, 1000).astype(jnp.int32) * 3 + jnp.arange(3, dtype=jnp.int32)[None, :]
    scores = jnp.where(usable, scores, -1)
    selected_entries = jnp.argmax(scores, axis=1).astype(jnp.int32)
    third = jnp.sum(jnp.where(jnp.arange(3, dtype=jnp.int32)[None, :] == selected_entries[:, None], candidates, 0), axis=1)
    return jnp.stack([tiles, tiles + signs * R, tiles + third], axis=1).astype(jnp.int32)


def block_levels(own_key, extent, shards, least, top_value):
    loudness, own = 1.0, jax.random.fold_in(own_key, 6)
    for position, parts in shards:
        steps = jnp.exp(jax.random.uniform(jax.random.fold_in(own, position), (parts,), jnp.float32, least / len(shards), top_value / len(shards)))
        loudness = loudness * jnp.repeat(steps, extent[position] // parts).reshape([-1 if axis == position else 1 for axis in range(len(extent))])
    return loudness


def noise(own_key, extent, scale, bound, shards=(), kind=jnp.bfloat16):
    array = scale * jax.random.normal(own_key, extent, jnp.float32)
    if shards:
        array = array * block_levels(own_key, extent, shards, -0.22, 0.18)
    return jnp.clip(array, -bound, bound).astype(kind)


def setup_inputs(seed: int = 0) -> dict:
    keys = jax.random.split(jax.random.key(seed), 16)
    return {
        "speeds": noise(keys[0], (SNAPS, NSEG), 1.0, 6.0, ((0, 128),), jnp.float32),
        "w_start": noise(keys[1], (C,), 1.0, 4.0, (), jnp.float32),
        "b_start": noise(keys[2], (C,), 0.5, 3.0, (), jnp.float32),
        "w_filter": noise(keys[3], (2, C, C), (2 * C) ** -0.5, 0.75),
        "b_filter": noise(keys[4], (C,), 0.5, 3.0, (), jnp.float32),
        "w_gate": noise(keys[5], (2, C, C), (2 * C) ** -0.5, 0.75),
        "b_gate": noise(keys[6], (C,), 0.5, 3.0, (), jnp.float32),
        "adj_cols": draw_adj_cols(jax.random.fold_in(keys[15], 71), 0),
        "adj_vals": noise(keys[8], (NTILES, K, TILE, TILE), (K * TILE) ** -0.5, 0.3125, ((0, 32),)),
        "w_mix": noise(keys[9], (C, 3 * C), (3 * C) ** -0.5, 0.625),
        "b_mix": noise(keys[10], (C,), 0.5, 3.0, (), jnp.float32),
        "w_skip": noise(keys[11], (SKIP, C), C ** -0.5, 1.0),
        "b_skip": noise(keys[12], (SKIP,), 0.5, 3.0, (), jnp.float32),
        "grad_res": noise(keys[13], (BATCH, OUTPUT_STEPS, C, NSEG), 1.0, 6.0, ((0, 4), (3, 32))),
        "grad_skip": noise(keys[14], (BATCH, SKIP, NSEG), 1.0, 6.0, ((0, 4), (2, 32))),
    }


HIGH_CHANNELS = lax.Precision.HIGHEST

def forward_spread(receptive_input, columns, block_list):
    summed_values = jnp.zeros(receptive_input.shape, jnp.float32)
    for column_vector in range(columns.shape[1]):
        selected_entries = jnp.take(receptive_input, columns[:, column_vector], axis=1)
        summed_values = summed_values + jnp.einsum('enb,ntb->ent', selected_entries, block_list[:, column_vector], precision=HIGH_CHANNELS)
    return summed_values

def backward_spread(receptive_input, columns, block_list):
    summed_values = jnp.zeros(receptive_input.shape, jnp.float32)
    for column_vector in range(columns.shape[1]):
        matrix_product = jnp.einsum('htg,tgd->htd', receptive_input, block_list[:, column_vector], precision=HIGH_CHANNELS)
        summed_values = summed_values.at[:, columns[:, column_vector]].add(matrix_product)
    return summed_values

def reference(speeds, w_start, b_start, w_filter, b_filter, w_gate, b_gate, adj_cols, adj_vals, w_mix, b_mix, w_skip, b_skip, grad_res, grad_skip):
    res_scale = 1.0 / math.sqrt(BATCH * OUTPUT_STEPS * NSEG)
    skip_scale = 1.0 / math.sqrt(BATCH * NSEG)
    wf = w_filter.astype(jnp.float32)
    wg = w_gate.astype(jnp.float32)
    wm = w_mix.astype(jnp.float32)
    wsk = w_skip.astype(jnp.float32)
    block_list = adj_vals.astype(jnp.float32)
    columns = adj_cols.astype(jnp.int32)
    series_all = speeds.reshape(BATCH, T_IN, NSEG)

    def tiled(arr):
        return arr.reshape(OUTPUT_STEPS * C, NTILES, TILE)

    def untiled(arr):
        return arr.reshape(OUTPUT_STEPS, C, NSEG)

    def sample_step(inputs):
        signal_series, cot_res, cot_skip = inputs
        hidden = (w_start[None, :, None] * signal_series[:, None, :] + b_start[None, :, None]).astype(jnp.bfloat16)
        hidden_function = hidden.astype(jnp.float32)
        lower = hidden_function[:OUTPUT_STEPS]
        upper_bound = hidden_function[DILATION_SIZE:]
        pre_f = jnp.einsum('oi,tin->ton', wf[0], lower, precision=HIGH_CHANNELS) + jnp.einsum('oi,tin->ton', wf[1], upper_bound, precision=HIGH_CHANNELS) + b_filter[None, :, None]
        pre_g = jnp.einsum('oi,tin->ton', wg[0], lower, precision=HIGH_CHANNELS) + jnp.einsum('oi,tin->ton', wg[1], upper_bound, precision=HIGH_CHANNELS) + b_gate[None, :, None]
        filter_act = jnp.tanh(pre_f)
        gate_act = jax.nn.sigmoid(pre_g)
        gated = (filter_act * gate_act).astype(jnp.bfloat16).astype(jnp.float32)
        hop_one = untiled(forward_spread(tiled(gated), columns, block_list)).astype(jnp.bfloat16).astype(jnp.float32)
        hop_two = untiled(forward_spread(tiled(hop_one), columns, block_list)).astype(jnp.bfloat16).astype(jnp.float32)
        mixed = jnp.einsum('oj,tjn->ton', wm[:, :C], gated, precision=HIGH_CHANNELS)
        mixed = mixed + jnp.einsum('oj,tjn->ton', wm[:, C:2 * C], hop_one, precision=HIGH_CHANNELS)
        mixed = mixed + jnp.einsum('oj,tjn->ton', wm[:, 2 * C:], hop_two, precision=HIGH_CHANNELS)
        res_row = (mixed + b_mix[None, :, None] + upper_bound).astype(jnp.bfloat16)
        last_step = gated[OUTPUT_STEPS - 1]
        skip_row = (jnp.einsum('sc,cn->sn', wsk, last_step, precision=HIGH_CHANNELS) + b_skip[:, None]).astype(jnp.bfloat16)
        cot_r = cot_res.astype(jnp.float32)
        cot_s = cot_skip.astype(jnp.float32)
        d_mix = jnp.concatenate([jnp.einsum('ton,tjn->oj', cot_r, operand, precision=HIGH_CHANNELS) for operand in (gated, hop_one, hop_two)], axis=1) * res_scale
        d_mix_b = lax.optimization_barrier(jnp.sum(cot_r, axis=(0, 2))) * res_scale
        back_mix = jnp.einsum('oj,ton->tjn', wm, cot_r, precision=HIGH_CHANNELS) * res_scale
        dz_two = back_mix[:, 2 * C:].astype(jnp.bfloat16).astype(jnp.float32)
        dz_one = (back_mix[:, C:2 * C] + untiled(backward_spread(tiled(dz_two), columns, block_list))).astype(jnp.bfloat16).astype(jnp.float32)
        dz_zero = back_mix[:, :C] + untiled(backward_spread(tiled(dz_one), columns, block_list))
        skip_back = jnp.einsum('sc,sn->cn', wsk, cot_s, precision=HIGH_CHANNELS) * skip_scale
        dz_zero = dz_zero.at[OUTPUT_STEPS - 1].add(skip_back)
        d_skip = jnp.einsum('sn,cn->sc', cot_s, last_step, precision=HIGH_CHANNELS) * skip_scale
        d_skip_b = lax.optimization_barrier(jnp.sum(cot_s, axis=1)) * skip_scale
        d_filt = (dz_zero * gate_act * (1.0 - filter_act * filter_act)).astype(jnp.bfloat16).astype(jnp.float32)
        d_gt = (dz_zero * filter_act * gate_act * (1.0 - gate_act)).astype(jnp.bfloat16).astype(jnp.float32)
        d_filter = jnp.stack([jnp.einsum('ton,tin->oi', d_filt, lower, precision=HIGH_CHANNELS), jnp.einsum('ton,tin->oi', d_filt, upper_bound, precision=HIGH_CHANNELS)])
        d_gate = jnp.stack([jnp.einsum('ton,tin->oi', d_gt, lower, precision=HIGH_CHANNELS), jnp.einsum('ton,tin->oi', d_gt, upper_bound, precision=HIGH_CHANNELS)])
        d_filter_b = lax.optimization_barrier(jnp.sum(d_filt, axis=(0, 2)))
        d_gate_b = lax.optimization_barrier(jnp.sum(d_gt, axis=(0, 2)))
        backward_low = jnp.einsum('oi,ton->tin', wf[0], d_filt, precision=HIGH_CHANNELS) + jnp.einsum('oi,ton->tin', wg[0], d_gt, precision=HIGH_CHANNELS)
        backward_high = jnp.einsum('oi,ton->tin', wf[1], d_filt, precision=HIGH_CHANNELS) + jnp.einsum('oi,ton->tin', wg[1], d_gt, precision=HIGH_CHANNELS) + cot_r * res_scale
        start_weight_gradient = lax.optimization_barrier(jnp.sum(backward_low * signal_series[:OUTPUT_STEPS, None, :], axis=(0, 2))) + lax.optimization_barrier(jnp.sum(backward_high * signal_series[DILATION_SIZE:, None, :], axis=(0, 2)))
        d_start_b = lax.optimization_barrier(jnp.sum(backward_low, axis=(0, 2))) + lax.optimization_barrier(jnp.sum(backward_high, axis=(0, 2)))
        return (res_row, skip_row, (start_weight_gradient, d_start_b, d_filter, d_filter_b, d_gate, d_gate_b, d_mix, d_mix_b, d_skip, d_skip_b))
    res_out, skip_out, grads = lax.map(sample_step, (series_all, grad_res, grad_skip))
    totals = [lax.optimization_barrier(jnp.sum(item, axis=0)) for item in grads]
    return (res_out, skip_out, totals[0], totals[1], totals[2], totals[3], totals[4], totals[5], totals[6], totals[7], totals[8], totals[9])
```

```python
import math

import jax
import jax.numpy as jnp
from jax import lax
from jax.experimental import pallas as pl
from jax.experimental.pallas import tpu as pltpu
from jax.sharding import PartitionSpec as P

C = 32
SKIP = 256
TILE = 128
DIL = 16
TOUT = 32
T_IN = 48
BR = 2
TILES = 4
W = TILES * TILE
PAIR = 2 * TILE
TG = 8
ROWS = TG * C
F32 = jnp.float32
BF16 = jnp.bfloat16
A0F, A1F, CF, A0G, A1G, CG, WS, BS, BM = range(9)
PAY = 104
VMEM_LIMIT = 40 * 1024 * 1024


def dot(a, b):
    return jnp.dot(a, b, preferred_element_type=F32)


def dot_nt(a, b):
    return lax.dot_general(a, b, (((1,), (1,)), ((), ())), preferred_element_type=F32)


def column(row):
    n = row.shape[1]
    r = lax.broadcasted_iota(jnp.int32, (n, n), 0)
    c = lax.broadcasted_iota(jnp.int32, (n, n), 1)
    return jnp.sum(jnp.where(r == c, jnp.broadcast_to(row, (n, n)), 0.0), axis=1, keepdims=True)


def block_diag(w):
    row = jnp.concatenate([w] * TG, axis=1)
    full = jnp.concatenate([row] * TG, axis=0)
    r = lax.broadcasted_iota(jnp.int32, (ROWS, ROWS), 0) // C
    c = lax.broadcasted_iota(jnp.int32, (ROWS, ROWS), 1) // C
    return jnp.where(r == c, full, 0.0)


def prep_kernel(
    cl, co, cr, ws, bs, wf, bf, wg, bg, wm, bm, wmt, vl, vo, vr, coef, mix, mixt, band, bandt
):
    wrow, brow = ws[...], bs[...]

    def put(i, col):
        coef[i * C : (i + 1) * C, :] = jnp.broadcast_to(col, (C, TILE))

    def lane_sum(m):
        return jnp.sum(m, axis=1, keepdims=True)

    for w, bias, base, scale in ((wf, bf, A0F, 1.0), (wg, bg, A0G, 0.5)):
        w0, w1 = w[0].astype(F32), w[1].astype(F32)
        put(base, lane_sum(w0 * wrow) * scale)
        put(base + 1, lane_sum(w1 * wrow) * scale)
        put(base + 2, (lane_sum((w0 + w1) * brow) + column(bias[...])) * scale)
    put(WS, column(wrow))
    put(BS, column(brow))
    put(BM, column(bm[...]))
    for h in range(3):
        mix[:, h * ROWS : (h + 1) * ROWS] = block_diag(
            wm[:, h * C : (h + 1) * C].astype(F32)
        ).astype(BF16)
        mixt[:, h * ROWS : (h + 1) * ROWS] = block_diag(
            wmt[h * C : (h + 1) * C, :].astype(F32)
        ).astype(BF16)

    band[...] = jnp.zeros_like(band)
    bandt[...] = jnp.zeros_like(bandt)
    base = lax.axis_index("seg") * TILES - TILES
    for src, (cols, vals) in enumerate(((cl, vl), (co, vo), (cr, vr))):

        def place(n, carry, src=src, cols=cols, vals=vals):
            r, k = n // 3, n % 3
            rel = cols[r, k] - base

            @pl.when(jnp.logical_and(rel >= 0, rel < 3 * TILES))
            def _():
                block = vals[r, k]
                at = pl.multiple_of(rel * TILE, TILE)
                row = pl.multiple_of((src * TILES + r) * TILE, TILE)
                band[pl.ds(row, TILE), pl.ds(at, TILE)] = block
                bandt[pl.ds(at, TILE), pl.ds(row, TILE)] = block.T

            return carry

        lax.fori_loop(0, TILES * 3, place, 0)


def two_hops(ext, one, band, p_one, p_two):
    for p in range(4):
        one[:, p * PAIR : (p + 1) * PAIR] = dot(
            ext[:, p * PAIR : (p + 3) * PAIR],
            band[p * PAIR : (p + 3) * PAIR, (p + 1) * PAIR : (p + 2) * PAIR],
        ).astype(BF16)
    for p in range(2):
        p_two(
            p,
            dot(
                one[:, p * PAIR : (p + 3) * PAIR],
                band[(p + 1) * PAIR : (p + 4) * PAIR, (p + 2) * PAIR : (p + 3) * PAIR],
            ).astype(BF16),
        )


def coefs(coef, *which):
    return [coef[i * C : (i + 1) * C, :] for i in which]


def forward_kernel(x0, x1, coef, mix, bandt, res, zext, one, stack):
    def step(t, carry):
        a0f, a1f, cf, a0g, a1g, cg = coefs(coef, A0F, A1F, CF, A0G, A1G, CG)
        lanes = pl.ds(pl.multiple_of(t * TILE, TILE), TILE)
        for k in range(TG):
            p = x0[0, k : k + 1, lanes]
            q = x1[0, k : k + 1, lanes]
            f = jnp.tanh(a0f * p + a1f * q + cf)
            g = 0.5 * jnp.tanh(a0g * p + a1g * q + cg) + 0.5
            zext[k * C : (k + 1) * C, lanes] = (f * g).astype(BF16)
        return carry

    lax.fori_loop(0, 3 * TILES, step, 0)
    stack[0:ROWS, :] = zext[:, W : 2 * W]

    def put(p, v):
        stack[2 * ROWS : 3 * ROWS, p * PAIR : (p + 1) * PAIR] = v

    two_hops(zext, one, bandt, None, put)
    stack[ROWS : 2 * ROWS, :] = one[:, PAIR : PAIR + W]
    mixed = dot(mix[...], stack[...])
    ws, bs, bm = coefs(coef, WS, BS, BM)
    bb = bs + bm
    for k in range(TG):
        for t in range(TILES):
            q = x1[0, k : k + 1, W + t * TILE : W + (t + 1) * TILE]
            r, lanes = slice(k * C, (k + 1) * C), slice(t * TILE, (t + 1) * TILE)
            res[r, lanes] = (mixed[r, lanes] + (ws * q + bb)).astype(BF16)


def backward_kernel(
    x0, x1, coef, mixt, wsk, wskt, bsk, band, gl, go, gr, gs,
    skip, pay, ext, one, stack, zb, dzs, acc, dmx, dsk,
):
    i = pl.program_id(0)
    last = i % 4 == 3
    res_scale = 1.0 / math.sqrt(8 * TOUT * 16384)
    skip_scale = 1.0 / math.sqrt(8 * 16384)

    @pl.when(i == 0)
    def _():
        acc[...] = jnp.zeros_like(acc)
        dmx[...] = jnp.zeros_like(dmx)
        dsk[...] = jnp.zeros_like(dsk)

    ext[:, 0:W] = gl[...]
    ext[:, W : 2 * W] = go[...]
    ext[:, 2 * W : 3 * W] = gr[...]
    stack[0:ROWS, :] = go[...]

    def put(p, v):
        stack[2 * ROWS : 3 * ROWS, p * PAIR : (p + 1) * PAIR] = v

    two_hops(ext, one, band, None, put)
    stack[ROWS : 2 * ROWS, :] = one[:, PAIR : PAIR + W]
    dzs[...] = dot(mixt[...], stack[...]) * res_scale

    @pl.when(last)
    def _():
        dzs[ROWS - C : ROWS, :] += dot(wskt[...], gs[0]) * skip_scale

    a0f, a1f, cf, a0g, a1g, cg = coefs(coef, A0F, A1F, CF, A0G, A1G, CG)
    sums = [acc[j] for j in range(8)]
    for k in range(TG):
        for t in range(TILES):
            r, lanes = slice(k * C, (k + 1) * C), slice(t * TILE, (t + 1) * TILE)
            p = x0[0, k : k + 1, W + t * TILE : W + (t + 1) * TILE]
            q = x1[0, k : k + 1, W + t * TILE : W + (t + 1) * TILE]
            f = jnp.tanh(a0f * p + a1f * q + cf)
            g = 0.5 * jnp.tanh(a0g * p + a1g * q + cg) + 0.5
            zb[r, lanes] = (f * g).astype(BF16)
            dg = dzs[r, lanes] * g
            df = dg * (1.0 - f * f)
            dgt = dg * f * (1.0 - g)
            e = go[r, lanes].astype(F32)
            for j, term in enumerate((df * p, df * q, df, dgt * p, dgt * q, dgt, e * q, e)):
                sums[j] = sums[j] + term
    for j in range(8):
        acc[j] = sums[j]
    dmx[...] += dot_nt(stack[...], zb[...])

    @pl.when(last)
    def _():
        z31 = zb[ROWS - C : ROWS, :]
        ones = jnp.ones((16, W), BF16)
        dsk[...] += dot_nt(jnp.concatenate([z31, ones], axis=0), gs[0])
        skip[0] = (dot(wsk[...], z31) + bsk[...]).astype(BF16)

    @pl.when(i == 7)
    def _():
        r = lax.broadcasted_iota(jnp.int32, (ROWS, ROWS), 0) // C
        c = lax.broadcasted_iota(jnp.int32, (ROWS, ROWS), 1) // C
        lane = lax.broadcasted_iota(jnp.int32, (C, TILE), 1)
        packed = jnp.zeros((C, TILE), F32)
        for h in range(3):
            m = jnp.where(r == c, dmx[h * ROWS : (h + 1) * ROWS, :], 0.0)
            v = m[0:C]
            for k in range(1, TG):
                v = v + m[k * C : (k + 1) * C]
            v = v[:, :TILE] + v[:, TILE:]
            v = v + pltpu.roll(v, 64, 1)
            v = v + pltpu.roll(v, 32, 1)
            packed = jnp.where(lane // C == h, v, packed)
        for j in range(8):
            s = jnp.sum(acc[j], axis=1, keepdims=True)
            packed = jnp.where(lane == 96 + j, s, packed)
        pay[0:C, :] = packed
        pay[C : 2 * C, :] = dsk[0:C, 0:TILE]
        pay[2 * C : 3 * C, :] = dsk[0:C, TILE:]
        sub = lax.broadcasted_iota(jnp.int32, (8, TILE), 0)
        pay[3 * C : PAY, :] = jnp.where(sub == 0, dsk[C : C + 8, 0:TILE], dsk[C : C + 8, TILE:])


def finish_kernel(
    p0, p1, p2, p3, ws, bs, wf, wg,
    swg, dsb, dfil, dfb, dgat, dgb, dmix, dmixb, dskip, dskipb,
):
    res_scale = 1.0 / math.sqrt(8 * TOUT * 16384)
    skip_scale = 1.0 / math.sqrt(8 * 16384)
    v = (p0[...] + p1[...]) + (p2[...] + p3[...])
    wrow, brow = ws[...], bs[...]
    head = v[0:C]
    rows = head.T
    uf0, uf1, fb, ug0, ug1, gb = (head[:, 96 + j : 97 + j] for j in range(6))
    dmix[...] = head[:, 0:96] * res_scale
    dfil[0] = uf0 * wrow + fb * brow
    dfil[1] = uf1 * wrow + fb * brow
    dgat[0] = ug0 * wrow + gb * brow
    dgat[1] = ug1 * wrow + gb * brow
    dfb[...] = rows[98:99]
    dgb[...] = rows[101:102]
    mb = rows[103:104] * res_scale
    dmixb[...] = mb
    f0, f1, g0, g1 = wf[0].astype(F32), wf[1].astype(F32), wg[0].astype(F32), wg[1].astype(F32)
    swg[...] = (
        jnp.sum(f0 * uf0 + f1 * uf1 + g0 * ug0 + g1 * ug1, axis=0, keepdims=True)
        + rows[102:103] * res_scale
    )
    dsb[...] = jnp.sum((f0 + f1) * fb + (g0 + g1) * gb, axis=0, keepdims=True) + mb
    dskip[0:TILE, :] = v[C : 2 * C].T * skip_scale
    dskip[TILE:, :] = v[2 * C : 3 * C].T * skip_scale
    dskipb[:, 0:TILE] = v[3 * C : 3 * C + 1] * skip_scale
    dskipb[:, TILE:] = v[3 * C + 1 : 3 * C + 2] * skip_scale


def neighbour(value, steps):
    count = lax.axis_size("seg")
    pairs = [(i, i + steps) for i in range(max(0, -steps), min(count, count - steps))]
    return lax.ppermute(value, "seg", pairs)


def seg_ring(value, shift):
    return lax.ppermute(value, "seg", [(i, shift(i)) for i in range(lax.axis_size("seg"))])


def whole(shape):
    return pl.BlockSpec(shape, lambda *_: (0,) * len(shape))


def params(**kw):
    return pltpu.CompilerParams(vmem_limit_bytes=VMEM_LIMIT, **kw)


VMEM = pl.BlockSpec(memory_space=pltpu.VMEM)
SMEM = pl.BlockSpec(memory_space=pltpu.SMEM)


def body(
    speeds, w_start, b_start, w_filter, b_filter, w_gate, b_gate, adj_cols, adj_vals,
    w_mix, b_mix, w_skip, b_skip, grad_res, grad_skip,
):
    rows = BR * TOUT * C
    grad = grad_res.reshape(rows, W)
    x = lax.all_to_all(speeds.astype(BF16), "seg", split_axis=1, concat_axis=0, tiled=True)
    grad_l, grad_r = neighbour(grad, 1), neighbour(grad, -1)
    vals_l, vals_r = neighbour(adj_vals, 1), neighbour(adj_vals, -1)
    cols_l, cols_r = neighbour(adj_cols, 1), neighbour(adj_cols, -1)
    x_l, x_r = neighbour(x, 1), neighbour(x, -1)
    xs = jnp.concatenate([x_l, x, x_r], axis=1).astype(F32).reshape(BR * T_IN // TG, TG, 3 * W)

    ws, bs = w_start.reshape(1, C), b_start.reshape(1, C)
    coef, mix, mixt, band, bandt = pl.pallas_call(
        prep_kernel,
        out_shape=(
            jax.ShapeDtypeStruct((9 * C, TILE), F32),
            jax.ShapeDtypeStruct((ROWS, 3 * ROWS), BF16),
            jax.ShapeDtypeStruct((ROWS, 3 * ROWS), BF16),
            jax.ShapeDtypeStruct((3 * W, 3 * W), BF16),
            jax.ShapeDtypeStruct((3 * W, 3 * W), BF16),
        ),
        in_specs=[SMEM] * 3 + [VMEM] * 12,
        out_specs=(VMEM,) * 5,
        compiler_params=params(),
        name="prep",
    )(
        cols_l, adj_cols, cols_r, ws, bs, w_filter, b_filter.reshape(1, C), w_gate,
        b_gate.reshape(1, C), w_mix, b_mix.reshape(1, C), w_mix.T, vals_l, adj_vals, vals_r,
    )

    early = pl.BlockSpec((1, TG, 3 * W), lambda i: ((i // 4) * 6 + i % 4, 0, 0))
    late = pl.BlockSpec((1, TG, 3 * W), lambda i: ((i // 4) * 6 + i % 4 + 2, 0, 0))
    slab = pl.BlockSpec((ROWS, W), lambda i: (i, 0))
    res = pl.pallas_call(
        forward_kernel,
        grid=(8,),
        out_shape=jax.ShapeDtypeStruct((rows, W), BF16),
        in_specs=[early, late, whole((9 * C, TILE)), whole((ROWS, 3 * ROWS)), whole((3 * W, 3 * W))],
        out_specs=slab,
        scratch_shapes=[
            pltpu.VMEM((ROWS, 3 * W), BF16),
            pltpu.VMEM((ROWS, 2 * W), BF16),
            pltpu.VMEM((3 * ROWS, W), BF16),
        ],
        compiler_params=params(),
        name="forward",
    )(xs, xs, coef, mix, bandt)

    per_sample = pl.BlockSpec((1, SKIP, W), lambda i: (i // 4, 0, 0))
    skip, pay = pl.pallas_call(
        backward_kernel,
        grid=(8,),
        out_shape=(
            jax.ShapeDtypeStruct((BR, SKIP, W), BF16),
            jax.ShapeDtypeStruct((PAY, TILE), F32),
        ),
        in_specs=[
            early, late, whole((9 * C, TILE)), whole((ROWS, 3 * ROWS)), whole((SKIP, C)),
            whole((C, SKIP)), whole((SKIP, 1)), whole((3 * W, 3 * W)), slab, slab, slab, per_sample,
        ],
        out_specs=(per_sample, whole((PAY, TILE))),
        scratch_shapes=[
            pltpu.VMEM((ROWS, 3 * W), BF16),
            pltpu.VMEM((ROWS, 2 * W), BF16),
            pltpu.VMEM((3 * ROWS, W), BF16),
            pltpu.VMEM((ROWS, W), BF16),
            pltpu.VMEM((ROWS, W), F32),
            pltpu.VMEM((8, C, TILE), F32),
            pltpu.VMEM((3 * ROWS, ROWS), F32),
            pltpu.VMEM((C + 16, SKIP), F32),
        ],
        compiler_params=params(),
        name="backward",
    )(
        xs, xs, coef, mixt, w_skip, w_skip.T, b_skip.reshape(SKIP, 1), band,
        grad_l, grad, grad_r, grad_skip,
    )

    v = pay
    v = v + seg_ring(v, lambda i: i ^ 1)
    v = v + sum(seg_ring(v, lambda i, k=k: (i // 8) * 8 + ((i // 2 + k) % 4) * 2 + i % 2) for k in (1, 2, 3))
    v = v + sum(seg_ring(v, lambda i, k=k: (i + 8 * k) % 32) for k in (1, 2, 3))
    others = [lax.ppermute(v, "rep", [(i, (i + k) % 4) for i in range(4)]) for k in (1, 2, 3)]

    row = jax.ShapeDtypeStruct((1, C), F32)
    taps = jax.ShapeDtypeStruct((2, C, C), F32)
    swg, dsb, dfil, dfb, dgat, dgb, dmix, dmixb, dskip, dskipb = pl.pallas_call(
        finish_kernel,
        out_shape=(
            row, row, taps, row, taps, row, jax.ShapeDtypeStruct((C, 3 * C), F32), row,
            jax.ShapeDtypeStruct((SKIP, C), F32), jax.ShapeDtypeStruct((1, SKIP), F32),
        ),
        in_specs=[VMEM] * 8,
        out_specs=(VMEM,) * 10,
        compiler_params=params(),
        name="finish",
    )(v, *others, ws, bs, w_filter, w_gate)
    vec = lambda a: a.reshape(-1)
    return (
        res.reshape(BR, TOUT, C, W), skip, vec(swg), vec(dsb), dfil, vec(dfb), dgat, vec(dgb),
        dmix, vec(dmixb), dskip, vec(dskipb),
    )


def solution(mesh):
    placed = (
        P(("rep", "seg"), None), P(), P(), P(), P(), P(), P(), P("seg", None),
        P("seg", None, None, None), P(), P(), P(), P(), P("rep", None, None, "seg"),
        P("rep", None, "seg"),
    )
    return jax.shard_map(
        body,
        mesh=mesh,
        in_specs=placed,
        out_specs=(P("rep", None, None, "seg"), P("rep", None, "seg")) + (P(),) * 10,
        check_vma=False,
    )
```

```python
import functools
import math

import jax
import jax.numpy as jnp
from jax import lax
from jax.experimental import pallas as pl
from jax.experimental.pallas import tpu as pltpu
from jax.sharding import PartitionSpec as P

C = 32
SKIP = 256
TILE = 128
DIL = 16
TOUT = 32
T_IN = 48
BR = 2
TILES = 4
W = TILES * TILE
PAIR = 2 * TILE
TG = 8
ROWS = TG * C
F32 = jnp.float32
BF16 = jnp.bfloat16
A0F, A1F, CF, A0G, A1G, CG, WS, BS, BM = range(9)
PAY = 104
VMEM_LIMIT = 40 * 1024 * 1024


def dot(a, b):
    return jnp.dot(a, b, preferred_element_type=F32)


def dot_nt(a, b):
    return lax.dot_general(a, b, (((1,), (1,)), ((), ())), preferred_element_type=F32)


def column(row):
    n = row.shape[1]
    r = lax.broadcasted_iota(jnp.int32, (n, n), 0)
    c = lax.broadcasted_iota(jnp.int32, (n, n), 1)
    return jnp.sum(jnp.where(r == c, jnp.broadcast_to(row, (n, n)), 0.0), axis=1, keepdims=True)


def block_diag(w):
    row = jnp.concatenate([w] * TG, axis=1)
    full = jnp.concatenate([row] * TG, axis=0)
    r = lax.broadcasted_iota(jnp.int32, (ROWS, ROWS), 0) // C
    c = lax.broadcasted_iota(jnp.int32, (ROWS, ROWS), 1) // C
    return jnp.where(r == c, full, 0.0)


def message_kernel(cols, speeds, msg, wide):
    wide[:, 0:W] = jnp.zeros((4, W), F32)
    wide[:, W + 16384 :] = jnp.zeros((4, W), F32)
    wide[0:3, W : W + 16384] = speeds[...]
    first = lax.axis_index("seg") * TILES
    offsets = jnp.concatenate(
        [
            jnp.broadcast_to((cols[t, k] - (first + t)).astype(F32), (4, TILE))
            for t in range(TILES)
            for k in range(3)
        ],
        axis=1,
    )
    row = lax.broadcasted_iota(jnp.int32, (4, 3 * W), 0)
    for d in range(32):
        msg[d] = jnp.where(row == 3, offsets, wide[:, d * W : (d + 3) * W]).astype(BF16)


def prep_kernel(
    ws, bs, wf, bf, wg, bg, wm, bm, wskt, bsk, vl, vo, vr, msg,
    coef, mix, mixt, wsk, bskc, band, bandt, xs,
):
    wrow, brow = ws[...], bs[...]

    def put(i, col):
        coef[i * C : (i + 1) * C, :] = jnp.broadcast_to(col, (C, TILE))

    def lane_sum(m):
        return jnp.sum(m, axis=1, keepdims=True)

    for w, bias, base, scale in ((wf, bf, A0F, 1.0), (wg, bg, A0G, 0.5)):
        w0, w1 = w[0].astype(F32), w[1].astype(F32)
        put(base, lane_sum(w0 * wrow) * scale)
        put(base + 1, lane_sum(w1 * wrow) * scale)
        put(base + 2, (lane_sum((w0 + w1) * brow) + column(bias[...])) * scale)
    put(WS, column(wrow))
    put(BS, column(brow))
    put(BM, column(bm[...]))
    for h in range(3):
        w = wm[:, h * C : (h + 1) * C].astype(F32)
        mix[:, h * ROWS : (h + 1) * ROWS] = block_diag(w).astype(BF16)
        mixt[:, h * ROWS : (h + 1) * ROWS] = block_diag(w.T).astype(BF16)
    wsk[...] = wskt[...].astype(F32).T.astype(BF16)
    bskc[...] = jnp.broadcast_to(column(bsk[...]), (SKIP, TILE))

    for i in range(32):
        xs[3 * i : 3 * i + 3, :] = msg[i].astype(F32)[0:3]

    def store(dst, row, col, v):
        j = col // 2 - 1
        at = row - 2 * j
        if 0 <= j < 4 and 0 <= at < 6:
            dst[j, at * TILE : (at + 1) * TILE, (col % 2) * TILE : (col % 2 + 1) * TILE] = v

    zero = jnp.zeros((TILE, TILE), BF16)
    for dst in (band, bandt):
        for j in range(4):
            dst[j, 0:TILE, TILE:] = zero
            dst[j, 5 * TILE :, 0:TILE] = zero
    seg = lax.axis_index("seg")
    for src, vals in enumerate((vl, vo, vr)):
        sender = jnp.clip(seg + src - 1, 0, 31)
        for t in range(TILES):
            m = src * TILES + t
            v0, v1, v2 = (vals[t, k] for k in range(3))
            u0, u1, u2 = v0.T, v1.T, v2.T

            def off(k, t=t, sender=sender):
                return msg[sender, :, (t * 3 + k) * TILE : (t * 3 + k + 1) * TILE].astype(F32)[3:4]

            o1, o2 = off(1), off(2)
            store(band, m, m, v0)
            store(bandt, m, m, u0)
            for o in (-2, -1, 1, 2):
                q = m + o
                if not 0 <= q < 12:
                    continue
                c2 = jnp.broadcast_to(jnp.where(o2 == o, 1.0, 0.0).astype(BF16), (TILE, TILE))
                v, u = c2 * v2, c2 * u2
                if abs(o) == 2:
                    c1 = jnp.broadcast_to(jnp.where(o1 == o, 1.0, 0.0).astype(BF16), (TILE, TILE))
                    v, u = v + c1 * v1, u + c1 * u1
                store(band, m, q, v)
                store(bandt, q, m, u)


def two_hops(ext, one, band, p_two):
    for p in range(4):
        one[:, p * PAIR : (p + 1) * PAIR] = dot(
            ext[:, p * PAIR : (p + 3) * PAIR], band[p]
        ).astype(BF16)
    for p in range(2):
        p_two(p, dot(one[:, p * PAIR : (p + 3) * PAIR], band[p + 1]).astype(BF16))


def coefs(coef, *which):
    return [coef[i * C : (i + 1) * C, :] for i in which]


def forward_kernel(base, xs, coef, mix, bandt, *refs):
    res, zext, one, stack = refs[-4:]
    i = pl.program_id(0) + base
    at = ((i // 4) * 6 + i % 4) * TG
    x0 = xs.at[pl.ds(pl.multiple_of(at, TG), TG)]
    x1 = xs.at[pl.ds(pl.multiple_of(at + DIL, TG), TG)]

    def step(t, carry):
        a0f, a1f, cf, a0g, a1g, cg = coefs(coef, A0F, A1F, CF, A0G, A1G, CG)
        lanes = pl.ds(pl.multiple_of(t * TILE, TILE), TILE)
        for k in range(TG):
            p = x0[k : k + 1, lanes]
            q = x1[k : k + 1, lanes]
            f = jnp.tanh(a0f * p + a1f * q + cf)
            g = 0.5 * jnp.tanh(a0g * p + a1g * q + cg) + 0.5
            zext[k * C : (k + 1) * C, lanes] = (f * g).astype(BF16)
        return carry

    lax.fori_loop(0, 3 * TILES, step, 0)
    stack[0:ROWS, :] = zext[:, W : 2 * W]

    def put(p, v):
        stack[2 * ROWS : 3 * ROWS, p * PAIR : (p + 1) * PAIR] = v

    two_hops(zext, one, bandt, put)
    stack[ROWS : 2 * ROWS, :] = one[:, PAIR : PAIR + W]
    mixed = dot(mix[...], stack[...])
    ws, bs, bm = coefs(coef, WS, BS, BM)
    bb = bs + bm
    for k in range(TG):
        for t in range(TILES):
            q = x1[k : k + 1, W + t * TILE : W + (t + 1) * TILE]
            r, lanes = slice(k * C, (k + 1) * C), slice(t * TILE, (t + 1) * TILE)
            res[r, lanes] = (mixed[r, lanes] + (ws * q + bb)).astype(BF16)


def backward_kernel(sample, xs, coef, mixt, wsk, wskt, bsk, band, gl, go, gr, gs, *refs):
    skip, pay, ext, one, stack, zb, dzs, acc, dmx, dsk = refs[-10:]
    i = pl.program_id(0)
    last = i == 3
    at = (sample * 6 + i) * TG
    x0 = xs.at[pl.ds(pl.multiple_of(at, TG), TG)]
    x1 = xs.at[pl.ds(pl.multiple_of(at + DIL, TG), TG)]
    res_scale = 1.0 / math.sqrt(8 * TOUT * 16384)
    skip_scale = 1.0 / math.sqrt(8 * 16384)

    @pl.when(i == 0)
    def _():
        acc[...] = jnp.zeros_like(acc)
        dmx[...] = jnp.zeros_like(dmx)
        dsk[...] = jnp.zeros_like(dsk)

    ext[:, 0:W] = gl[...]
    ext[:, W : 2 * W] = go[...]
    ext[:, 2 * W : 3 * W] = gr[...]
    stack[0:ROWS, :] = go[...]

    def put(p, v):
        stack[2 * ROWS : 3 * ROWS, p * PAIR : (p + 1) * PAIR] = v

    two_hops(ext, one, band, put)
    stack[ROWS : 2 * ROWS, :] = one[:, PAIR : PAIR + W]
    dzs[...] = dot(mixt[...], stack[...]) * res_scale

    @pl.when(last)
    def _():
        dzs[ROWS - C : ROWS, :] += dot(wskt[...], gs[0]) * skip_scale

    a0f, a1f, cf, a0g, a1g, cg = coefs(coef, A0F, A1F, CF, A0G, A1G, CG)
    sums = [acc[j] for j in range(8)]
    for k in range(TG):
        for t in range(TILES):
            r, lanes = slice(k * C, (k + 1) * C), slice(t * TILE, (t + 1) * TILE)
            p = x0[k : k + 1, W + t * TILE : W + (t + 1) * TILE]
            q = x1[k : k + 1, W + t * TILE : W + (t + 1) * TILE]
            f = jnp.tanh(a0f * p + a1f * q + cf)
            g = 0.5 * jnp.tanh(a0g * p + a1g * q + cg) + 0.5
            zb[r, lanes] = (f * g).astype(BF16)
            dg = dzs[r, lanes] * g
            df = dg * (1.0 - f * f)
            dgt = dg * f * (1.0 - g)
            e = go[r, lanes].astype(F32)
            for j, term in enumerate((df * p, df * q, df, dgt * p, dgt * q, dgt, e * q, e)):
                sums[j] = sums[j] + term
    for j in range(8):
        acc[j] = sums[j]
    dmx[...] += dot_nt(stack[...], zb[...])

    @pl.when(last)
    def _():
        z31 = zb[ROWS - C : ROWS, :]
        ones = jnp.ones((16, W), BF16)
        dsk[...] += dot_nt(jnp.concatenate([z31, ones], axis=0), gs[0])
        bias = jnp.concatenate([bsk[...]] * TILES, axis=1)
        skip[0] = (dot(wsk[...], z31) + bias).astype(BF16)

    @pl.when(last)
    def _():
        r = lax.broadcasted_iota(jnp.int32, (ROWS, ROWS), 0) // C
        c = lax.broadcasted_iota(jnp.int32, (ROWS, ROWS), 1) // C
        lane = lax.broadcasted_iota(jnp.int32, (C, TILE), 1)
        packed = jnp.zeros((C, TILE), F32)
        for h in range(3):
            m = jnp.where(r == c, dmx[h * ROWS : (h + 1) * ROWS, :], 0.0)
            v = m[0:C]
            for k in range(1, TG):
                v = v + m[k * C : (k + 1) * C]
            v = v[:, :TILE] + v[:, TILE:]
            v = v + pltpu.roll(v, 64, 1)
            v = v + pltpu.roll(v, 32, 1)
            packed = jnp.where(lane // C == h, v, packed)
        for j in range(8):
            s = jnp.sum(acc[j], axis=1, keepdims=True)
            packed = jnp.where(lane == 96 + j, s, packed)
        pay[0:C, :] = packed
        pay[C : 2 * C, :] = dsk[0:C, 0:TILE]
        pay[2 * C : 3 * C, :] = dsk[0:C, TILE:]
        sub = lax.broadcasted_iota(jnp.int32, (8, TILE), 0)
        pay[3 * C : PAY, :] = jnp.where(sub == 0, dsk[C : C + 8, 0:TILE], dsk[C : C + 8, TILE:])


def finish_kernel(
    p0, p1, p2, p3, ws, bs, wf, wg,
    swg, dsb, dfil, dfb, dgat, dgb, dmix, dmixb, dskip, dskipb,
):
    res_scale = 1.0 / math.sqrt(8 * TOUT * 16384)
    skip_scale = 1.0 / math.sqrt(8 * 16384)
    v = (p0[...] + p1[...]) + (p2[...] + p3[...])
    wrow, brow = ws[...], bs[...]
    head = v[0:C]
    rows = head.T
    uf0, uf1, fb, ug0, ug1, gb = (head[:, 96 + j : 97 + j] for j in range(6))
    dmix[...] = head[:, 0:96] * res_scale
    dfil[0] = uf0 * wrow + fb * brow
    dfil[1] = uf1 * wrow + fb * brow
    dgat[0] = ug0 * wrow + gb * brow
    dgat[1] = ug1 * wrow + gb * brow
    dfb[...] = rows[98:99]
    dgb[...] = rows[101:102]
    mb = rows[103:104] * res_scale
    dmixb[...] = mb
    f0, f1, g0, g1 = wf[0].astype(F32), wf[1].astype(F32), wg[0].astype(F32), wg[1].astype(F32)
    swg[...] = (
        jnp.sum(f0 * uf0 + f1 * uf1 + g0 * ug0 + g1 * ug1, axis=0, keepdims=True)
        + rows[102:103] * res_scale
    )
    dsb[...] = jnp.sum((f0 + f1) * fb + (g0 + g1) * gb, axis=0, keepdims=True) + mb
    dskip[:, 0:TILE] = v[C : 2 * C] * skip_scale
    dskip[:, TILE:] = v[2 * C : 3 * C] * skip_scale
    dskipb[:, 0:TILE] = v[3 * C : 3 * C + 1] * skip_scale
    dskipb[:, TILE:] = v[3 * C + 1 : 3 * C + 2] * skip_scale


def neighbour(value, steps):
    count = lax.axis_size("seg")
    pairs = [(i, i + steps) for i in range(max(0, -steps), min(count, count - steps))]
    return lax.ppermute(value, "seg", pairs)


def seg_ring(value, shift):
    return lax.ppermute(value, "seg", [(i, shift(i)) for i in range(lax.axis_size("seg"))])


def whole(shape):
    return pl.BlockSpec(shape, lambda *_: (0,) * len(shape))


def params(**kw):
    return pltpu.CompilerParams(vmem_limit_bytes=VMEM_LIMIT, **kw)


VMEM = pl.BlockSpec(memory_space=pltpu.VMEM)
ANY = pl.BlockSpec(memory_space=pl.ANY)


def forward_call(base, count, xs, coef, mix, bandt, before):
    more = [] if before is None else [before]
    return pl.pallas_call(
        functools.partial(forward_kernel, base),
        grid=(count,),
        out_shape=jax.ShapeDtypeStruct((BR * TOUT * C, W), BF16),
        in_specs=[VMEM] * 4 + [ANY] * len(more),
        out_specs=pl.BlockSpec((ROWS, W), lambda i: (i + base, 0)),
        scratch_shapes=[
            pltpu.VMEM((ROWS, 3 * W), BF16),
            pltpu.VMEM((ROWS, 2 * W), BF16),
            pltpu.VMEM((3 * ROWS, W), BF16),
        ],
        input_output_aliases={4: 0} if more else {},
        compiler_params=params(),
        name="forward",
    )(xs, coef, mix, bandt, *more)


def backward_call(sample, xs, coef, mixt, wsk, wskt, bsk, band, gl, go, gr, gs, before):
    more = [] if before is None else [before]
    slab = pl.BlockSpec((ROWS, W), lambda i: (i, 0))
    own = pl.BlockSpec((ROWS, W), lambda i: (i + 4 * sample, 0))
    per_sample = pl.BlockSpec((1, SKIP, W), lambda i: (sample, 0, 0))
    return pl.pallas_call(
        functools.partial(backward_kernel, sample),
        grid=(4,),
        out_shape=(
            jax.ShapeDtypeStruct((BR, SKIP, W), BF16),
            jax.ShapeDtypeStruct((PAY, TILE), F32),
        ),
        in_specs=[VMEM] * 7 + [slab, own, slab, per_sample] + [ANY] * len(more),
        out_specs=(per_sample, whole((PAY, TILE))),
        scratch_shapes=[
            pltpu.VMEM((ROWS, 3 * W), BF16),
            pltpu.VMEM((ROWS, 2 * W), BF16),
            pltpu.VMEM((3 * ROWS, W), BF16),
            pltpu.VMEM((ROWS, W), BF16),
            pltpu.VMEM((ROWS, W), F32),
            pltpu.VMEM((8, C, TILE), F32),
            pltpu.VMEM((3 * ROWS, ROWS), F32),
            pltpu.VMEM((C + 16, SKIP), F32),
        ],
        input_output_aliases={11: 0} if more else {},
        compiler_params=params(),
        name="backward",
    )(xs, coef, mixt, wsk, wskt, bsk, band, gl, go, gr, gs, *more)


def send(speeds, cols):
    return pl.pallas_call(
        message_kernel,
        grid=(1,),
        out_shape=jax.ShapeDtypeStruct((32, 4, 3 * W), BF16),
        in_specs=[
            pl.BlockSpec((TILES, 3), lambda i: (0, 0), memory_space=pltpu.SMEM),
            whole((3, 16384)),
        ],
        out_specs=VMEM,
        scratch_shapes=[pltpu.VMEM((4, 16384 + 2 * W), F32)],
        compiler_params=params(),
        name="message",
    )(cols, speeds)


def prepare(msg, vals, w_start, b_start, w_filter, b_filter, w_gate, b_gate, w_mix, b_mix, w_skip, b_skip):
    row = lambda a: a.reshape(1, -1)
    small = [
        row(w_start), row(b_start), w_filter, row(b_filter), w_gate, row(b_gate), w_mix, row(b_mix),
        w_skip.T, row(b_skip), *vals,
    ]
    return pl.pallas_call(
        prep_kernel,
        grid=(1,),
        out_shape=(
            jax.ShapeDtypeStruct((9 * C, TILE), F32),
            jax.ShapeDtypeStruct((ROWS, 3 * ROWS), BF16),
            jax.ShapeDtypeStruct((ROWS, 3 * ROWS), BF16),
            jax.ShapeDtypeStruct((SKIP, C), BF16),
            jax.ShapeDtypeStruct((SKIP, TILE), F32),
            jax.ShapeDtypeStruct((4, 3 * PAIR, PAIR), BF16),
            jax.ShapeDtypeStruct((4, 3 * PAIR, PAIR), BF16),
            jax.ShapeDtypeStruct((BR * T_IN, 3 * W), F32),
        ),
        in_specs=[whole(a.shape) for a in small] + [VMEM],
        out_specs=(VMEM,) * 8,
        compiler_params=params(),
        name="prep",
    )(*small, msg)


def body(
    speeds, w_start, b_start, w_filter, b_filter, w_gate, b_gate, adj_cols, adj_vals,
    w_mix, b_mix, w_skip, b_skip, grad_res, grad_skip,
):
    barrier = lax.optimization_barrier
    half = TOUT * C
    grad = grad_res.reshape(BR * half, W)
    vals = (neighbour(adj_vals, 1), adj_vals, neighbour(adj_vals, -1))
    msg = lax.all_to_all(send(speeds, adj_cols), "seg", split_axis=0, concat_axis=0, tiled=True)
    first = grad[:half]
    msg, first = barrier((msg, first))
    halo0 = neighbour(first, 1), neighbour(first, -1)
    coef, mix, mixt, wsk, bsk, band, bandt, xs = prepare(
        msg, vals, w_start, b_start, w_filter, b_filter, w_gate, b_gate, w_mix, b_mix, w_skip, b_skip
    )
    xs, second = barrier((xs, grad[half:]))
    halo1 = neighbour(second, 1), neighbour(second, -1)

    common = (coef, mixt, wsk, w_skip.T, bsk, band)
    skip, pay0 = backward_call(0, xs, *common, halo0[0], grad, halo0[1], grad_skip, None)
    pay0, xs = barrier((pay0, xs))
    res = forward_call(0, 3, xs, coef, mix, bandt, None)
    res, xs = barrier((res, xs))
    skip, pay1 = backward_call(1, xs, *common, halo1[0], grad, halo1[1], grad_skip, skip)

    v = pay0 + pay1
    v = v + seg_ring(v, lambda i: i ^ 1)

    def forward(base, count, v, before):
        v, xs_now = barrier((v, xs))
        return v, forward_call(base, count, xs_now, coef, mix, bandt, before)

    v, res = forward(3, 2, v, res)
    v = v + sum(seg_ring(v, lambda i, k=k: (i // 8) * 8 + ((i // 2 + k) % 4) * 2 + i % 2) for k in (1, 2, 3))
    v, res = barrier((v, res))
    v, res = forward(5, 2, v, res)
    v = v + sum(seg_ring(v, lambda i, k=k: (i + 8 * k) % 32) for k in (1, 2, 3))
    v, res = barrier((v, res))
    v, res = forward(7, 1, v, res)
    others = [lax.ppermute(v, "rep", [(i, (i + k) % 4) for i in range(4)]) for k in (1, 2, 3)]

    row = jax.ShapeDtypeStruct((1, C), F32)
    taps = jax.ShapeDtypeStruct((2, C, C), F32)
    small = (v, *others, w_start.reshape(1, C), b_start.reshape(1, C), w_filter, w_gate)
    swg, dsb, dfil, dfb, dgat, dgb, dmix, dmixb, dskip, dskipb = pl.pallas_call(
        finish_kernel,
        grid=(1,),
        out_shape=(
            row, row, taps, row, taps, row, jax.ShapeDtypeStruct((C, 3 * C), F32), row,
            jax.ShapeDtypeStruct((C, SKIP), F32), jax.ShapeDtypeStruct((1, SKIP), F32),
        ),
        in_specs=[whole(a.shape) for a in small],
        out_specs=(whole((1, C)), whole((1, C)), whole((2, C, C)), whole((1, C)), whole((2, C, C)),
                   whole((1, C)), whole((C, 3 * C)), whole((1, C)), whole((C, SKIP)), whole((1, SKIP))),
        compiler_params=params(),
        name="finish",
    )(*small)
    vec = lambda a: a.reshape(-1)
    return (
        res.reshape(BR, TOUT, C, W), skip, vec(swg), vec(dsb), dfil, vec(dfb), dgat, vec(dgb),
        dmix, vec(dmixb), dskip.T, vec(dskipb),
    )


def solution(mesh):
    placed = (
        P(("rep", "seg"), None), P(), P(), P(), P(), P(), P(), P("seg", None),
        P("seg", None, None, None), P(), P(), P(), P(), P("rep", None, None, "seg"),
        P("rep", None, "seg"),
    )
    return jax.shard_map(
        body,
        mesh=mesh,
        in_specs=placed,
        out_specs=(P("rep", None, None, "seg"), P("rep", None, "seg")) + (P(),) * 10,
        check_vma=False,
    )
```

```python
import functools
import math

import jax
import jax.numpy as jnp
from jax import lax
from jax.experimental import pallas as pl
from jax.experimental.pallas import tpu as pltpu
from jax.sharding import PartitionSpec as P

C = 32
SKIP = 256
TILE = 128
DIL = 16
TOUT = 32
T_IN = 48
BR = 2
TILES = 4
W = TILES * TILE
PAIR = 2 * TILE
TG = 8
ROWS = TG * C
F32 = jnp.float32
BF16 = jnp.bfloat16
A0F, A1F, CF, A0G, A1G, CG, WS, BS, BM = range(9)
PAY = 104
RES_SCALE = 1.0 / math.sqrt(8 * TOUT * 16384)
SKIP_SCALE = 1.0 / math.sqrt(8 * 16384)
VMEM_LIMIT = 40 * 1024 * 1024


def dot(a, b):
    return jnp.dot(a, b, preferred_element_type=F32)


def dot_nt(a, b):
    return lax.dot_general(a, b, (((1,), (1,)), ((), ())), preferred_element_type=F32)


def column(row):
    n = row.shape[1]
    r = lax.broadcasted_iota(jnp.int32, (n, n), 0)
    c = lax.broadcasted_iota(jnp.int32, (n, n), 1)
    return jnp.sum(jnp.where(r == c, jnp.broadcast_to(row, (n, n)), 0.0), axis=1, keepdims=True)


def block_diag(w):
    row = jnp.concatenate([w] * TG, axis=1)
    full = jnp.concatenate([row] * TG, axis=0)
    r = lax.broadcasted_iota(jnp.int32, (ROWS, ROWS), 0) // C
    c = lax.broadcasted_iota(jnp.int32, (ROWS, ROWS), 1) // C
    return jnp.where(r == c, full, 0.0)


def message_kernel(cols_hbm, speeds, grad, msg, first, second, cols, rows, wide, stage, sems):
    half = first.shape[0]
    loads = [
        pltpu.make_async_copy(src, dst, sems.at[n])
        for n, (src, dst) in enumerate(
            (
                (speeds, rows),
                (cols_hbm, cols),
                (grad.at[pl.ds(0, half)], stage.at[0]),
                (grad.at[pl.ds(half, half)], stage.at[1]),
            )
        )
    ]
    stores = [
        pltpu.make_async_copy(stage.at[n], dst, sems.at[4 + n])
        for n, dst in enumerate((first, second))
    ]
    for copy in loads:
        copy.start()
    wide[:, 0:W] = jnp.zeros((4, W), F32)
    wide[:, W + 16384 :] = jnp.zeros((4, W), F32)
    loads[0].wait()
    loads[1].wait()
    wide[0:3, W : W + 16384] = rows[...]
    base = lax.axis_index("seg") * TILES
    offsets = jnp.concatenate(
        [
            jnp.broadcast_to((cols[t, k] - (base + t)).astype(F32), (4, TILE))
            for t in range(TILES)
            for k in range(3)
        ],
        axis=1,
    )
    row = lax.broadcasted_iota(jnp.int32, (4, 3 * W), 0)
    loads[2].wait()
    stores[0].start()
    for d in range(32):
        msg[d] = jnp.where(row == 3, offsets, wide[:, d * W : (d + 3) * W]).astype(BF16)
    loads[3].wait()
    stores[1].start()
    stores[0].wait()
    stores[1].wait()


def prep_kernel(
    ws, bs, wf, bf, wg, bg, wm, bm, wskt, bsk, vl, vo, vr, msg,
    coef, mix, mixt, wsk, bskc, band, bandt, xs,
):
    wrow, brow = ws[...], bs[...]

    def put(i, col):
        coef[i * C : (i + 1) * C, :] = jnp.broadcast_to(col, (C, TILE))

    def lane_sum(m):
        return jnp.sum(m, axis=1, keepdims=True)

    for w, bias, base, scale in ((wf, bf, A0F, 1.0), (wg, bg, A0G, 0.5)):
        w0, w1 = w[0].astype(F32), w[1].astype(F32)
        put(base, lane_sum(w0 * wrow) * scale)
        put(base + 1, lane_sum(w1 * wrow) * scale)
        put(base + 2, (lane_sum((w0 + w1) * brow) + column(bias[...])) * scale)
    put(WS, column(wrow))
    put(BS, column(brow))
    put(BM, column(bm[...]))
    for h in range(3):
        w = wm[:, h * C : (h + 1) * C].astype(F32)
        mix[:, h * ROWS : (h + 1) * ROWS] = block_diag(w * 0.5).astype(BF16)
        mixt[:, h * ROWS : (h + 1) * ROWS] = block_diag(w.T).astype(BF16)
    wsk[...] = (wskt[...].astype(F32) * 0.5).T.astype(BF16)
    bskc[...] = jnp.broadcast_to(column(bsk[...]), (SKIP, TILE))

    for i in range(32):
        xs[3 * i : 3 * i + 3, :] = msg[i].astype(F32)[0:3]

    def store(dst, row, col, v):
        j = col // 2 - 1
        at = row - 2 * j
        if 0 <= j < 4 and 0 <= at < 6:
            dst[j, at * TILE : (at + 1) * TILE, (col % 2) * TILE : (col % 2 + 1) * TILE] = v

    zero = jnp.zeros((TILE, TILE), BF16)
    for dst in (band, bandt):
        for j in range(4):
            dst[j, 0:TILE, TILE:] = zero
            dst[j, 5 * TILE :, 0:TILE] = zero
    seg = lax.axis_index("seg")
    for src, vals in enumerate((vl, vo, vr)):
        sender = jnp.clip(seg + src - 1, 0, 31)
        for t in range(TILES):
            m = src * TILES + t
            v0, v1, v2 = (vals[t, k] for k in range(3))
            u0, u1, u2 = v0.T, v1.T, v2.T

            def off(k, t=t, sender=sender):
                return msg[sender, :, (t * 3 + k) * TILE : (t * 3 + k + 1) * TILE].astype(F32)[3:4]

            o1, o2 = off(1), off(2)
            store(band, m, m, v0)
            store(bandt, m, m, u0)
            for o in (-2, -1, 1, 2):
                q = m + o
                if not 0 <= q < 12:
                    continue
                c2 = jnp.broadcast_to(jnp.where(o2 == o, 1.0, 0.0).astype(BF16), (TILE, TILE))
                v, u = c2 * v2, c2 * u2
                if abs(o) == 2:
                    c1 = jnp.broadcast_to(jnp.where(o1 == o, 1.0, 0.0).astype(BF16), (TILE, TILE))
                    v, u = v + c1 * v1, u + c1 * u1
                store(band, m, q, v)
                store(bandt, q, m, u)


def hops(ext, one, band, put, between):
    for p in range(4):
        one[:, p * PAIR : (p + 1) * PAIR] = dot(
            ext[:, p * PAIR : (p + 3) * PAIR], band[p]
        ).astype(BF16)
        between()
    for p in range(2):
        put(p, dot(one[:, p * PAIR : (p + 3) * PAIR], band[p + 1]).astype(BF16))
        between()


def coefs(coef, *which):
    return [coef[i * C : (i + 1) * C, :] for i in which]


def spread(bodies, slots):
    queue = list(bodies)
    share = -(-len(queue) // slots)

    def emit():
        for _ in range(min(share, len(queue))):
            queue.pop(0)()

    return emit


def lane_tile(t):
    return slice(t * TILE, (t + 1) * TILE)


def slab_rows(k):
    return slice(k * C, (k + 1) * C)


def gates(coef, p, q):
    a0f, a1f, cf, a0g, a1g, cg = coefs(coef, A0F, A1F, CF, A0G, A1G, CG)
    return jnp.tanh(a0f * p + a1f * q + cf), jnp.tanh(a0g * p + a1g * q + cg) + 1.0


def forward_kernel(base, count, xs, coef, mix, bandt, zown, *refs):
    res, ahead, zext, one, stack = refs[-5:]
    i = pl.program_id(0)

    def at(step):
        row = ((step // 4) * 6 + step % 4) * TG
        return (
            xs.at[pl.ds(pl.multiple_of(row, TG), TG)],
            xs.at[pl.ds(pl.multiple_of(row + DIL, TG), TG)],
        )

    halo = [t for t in range(12) if not 4 <= t < 8]

    def look_ahead(x0, x1, k, n):
        def emit():
            lanes = lane_tile(halo[n])
            f, u = gates(coef, x0[k : k + 1, lanes], x1[k : k + 1, lanes])
            ahead[slab_rows(k), lane_tile(n)] = (f * u).astype(BF16)

        return emit

    @pl.when(i == 0)
    def _():
        x0, x1 = at(i + base)
        for k in range(TG):
            for n in range(8):
                look_ahead(x0, x1, k, n)()

    zext[:, 0:W] = ahead[:, 0:W]
    zext[:, W : 2 * W] = zown[...]
    zext[:, 2 * W : 3 * W] = ahead[:, W : 2 * W]
    stack[0:ROWS, :] = zown[...]
    n0, n1 = at(jnp.minimum(i + 1, count - 1) + base)
    emit = spread([look_ahead(n0, n1, k, n) for k in range(TG) for n in range(8)], 6)

    def put(p, v):
        stack[2 * ROWS : 3 * ROWS, p * PAIR : (p + 1) * PAIR] = v

    hops(zext, one, bandt, put, emit)
    stack[ROWS : 2 * ROWS, :] = one[:, PAIR : PAIR + W]
    mixed = dot(mix[...], stack[...])
    ws, bs, bm = coefs(coef, WS, BS, BM)
    bb = bs + bm
    x1 = at(i + base)[1]
    for k in range(TG):
        for t in range(TILES):
            q = x1[k : k + 1, W + t * TILE : W + (t + 1) * TILE]
            r, lanes = slab_rows(k), lane_tile(t)
            res[r, lanes] = (mixed[r, lanes] + (ws * q + bb)).astype(BF16)


def backward_kernel(sample, xs, coef, mixt, wsk, wskt, bsk, band, gl, go, gr, gs, *refs):
    skip, pay, zb, ext, one, stack, dzs, fs, us, acc, dmx, dsk, extra = refs[-13:]
    i = pl.program_id(0)
    last = i == 3
    at = (sample * 6 + i) * TG
    x0 = xs.at[pl.ds(pl.multiple_of(at, TG), TG)]
    x1 = xs.at[pl.ds(pl.multiple_of(at + DIL, TG), TG)]

    @pl.when(i == 0)
    def _():
        acc[...] = jnp.zeros_like(acc)
        dmx[...] = jnp.zeros_like(dmx)
        extra[...] = jnp.zeros_like(extra)

    @pl.when(last)
    def _():
        extra[...] = dot(wskt[...], gs[0]) * (SKIP_SCALE / RES_SCALE)

    ext[:, 0:W] = gl[...]
    ext[:, W : 2 * W] = go[...]
    ext[:, 2 * W : 3 * W] = gr[...]
    stack[0:ROWS, :] = go[...]

    def rows_of(k, t):
        lanes = slice(W + t * TILE, W + (t + 1) * TILE)
        return x0[k : k + 1, lanes], x1[k : k + 1, lanes]

    def gate(k, t):
        def emit():
            r, lanes = slab_rows(k), lane_tile(t)
            f, u = gates(coef, *rows_of(k, t))
            fs[r, lanes] = f
            us[r, lanes] = u
            zb[r, lanes] = (f * u).astype(BF16)

        return emit

    def put(p, v):
        stack[2 * ROWS : 3 * ROWS, p * PAIR : (p + 1) * PAIR] = v

    hops(ext, one, band, put, spread([gate(k, t) for k in range(TG) for t in range(TILES)], 6))
    stack[ROWS : 2 * ROWS, :] = one[:, PAIR : PAIR + W]
    dzs[...] = dot(mixt[...], stack[...])
    dzs[ROWS - C : ROWS, :] += extra[...]

    sums = [acc[j] for j in range(8)]

    def local(k, t):
        def emit():
            r, lanes = slab_rows(k), lane_tile(t)
            p, q = rows_of(k, t)
            f, u = fs[r, lanes], us[r, lanes]
            s = dzs[r, lanes] * u
            df = s * (1.0 - f * f)
            dgt = (s * f) * (2.0 - u)
            e = go[r, lanes].astype(F32)
            for j, term in enumerate((df * p, df * q, df, dgt * p, dgt * q, dgt, e * q, e)):
                sums[j] = sums[j] + term

        return emit

    emit = spread([local(k, t) for k in range(TG) for t in range(TILES)], 3)
    for h in range(3):
        part = slice(h * ROWS, (h + 1) * ROWS)
        dmx[part, :] += dot_nt(stack[part, :], zb[...])
        emit()
    for j in range(8):
        acc[j] = sums[j]

    @pl.when(last)
    def _():
        z31 = zb[ROWS - C : ROWS, :]
        twos = jnp.full((16, W), 2.0, BF16)
        dsk[...] = dot_nt(jnp.concatenate([z31, twos], axis=0), gs[0])
        bias = jnp.concatenate([bsk[...]] * TILES, axis=1)
        skip[0] = (dot(wsk[...], z31) + bias).astype(BF16)

        r = lax.broadcasted_iota(jnp.int32, (ROWS, ROWS), 0) // C
        c = lax.broadcasted_iota(jnp.int32, (ROWS, ROWS), 1) // C
        lane = lax.broadcasted_iota(jnp.int32, (C, TILE), 1)
        packed = jnp.zeros((C, TILE), F32)
        for h in range(3):
            m = jnp.where(r == c, dmx[h * ROWS : (h + 1) * ROWS, :], 0.0)
            v = m[0:C]
            for k in range(1, TG):
                v = v + m[k * C : (k + 1) * C]
            v = v[:, :TILE] + v[:, TILE:]
            v = v + pltpu.roll(v, 64, 1)
            v = v + pltpu.roll(v, 32, 1)
            packed = jnp.where(lane // C == h, v, packed)
        scales = (0.5,) * 3 + (0.25,) * 3 + (1.0,) * 2
        packed = packed * (0.5 * RES_SCALE)
        for j in range(8):
            s = jnp.sum(acc[j], axis=1, keepdims=True) * (scales[j] * RES_SCALE)
            packed = jnp.where(lane == 96 + j, s, packed)
        pay[0:C, :] = packed
        pay[C : 2 * C, :] = dsk[0:C, 0:TILE] * (0.5 * SKIP_SCALE)
        pay[2 * C : 3 * C, :] = dsk[0:C, TILE:] * (0.5 * SKIP_SCALE)
        sub = lax.broadcasted_iota(jnp.int32, (8, TILE), 0)
        pay[3 * C : PAY, :] = jnp.where(
            sub == 0, dsk[C : C + 8, 0:TILE], dsk[C : C + 8, TILE:]
        ) * (0.5 * SKIP_SCALE)


def finish_kernel(
    p0, p1, p2, p3, ws, bs, wf, wg,
    swg, dsb, dfil, dfb, dgat, dgb, dmix, dmixb, dskip, dskipb,
):
    v = (p0[...] + p1[...]) + (p2[...] + p3[...])
    wrow, brow = ws[...], bs[...]
    head = v[0:C]
    rows = head.T
    uf0, uf1, fb, ug0, ug1, gb = (head[:, 96 + j : 97 + j] for j in range(6))
    dmix[...] = head[:, 0:96]
    dfil[0] = uf0 * wrow + fb * brow
    dfil[1] = uf1 * wrow + fb * brow
    dgat[0] = ug0 * wrow + gb * brow
    dgat[1] = ug1 * wrow + gb * brow
    dfb[...] = rows[98:99]
    dgb[...] = rows[101:102]
    mb = rows[103:104]
    dmixb[...] = mb
    f0, f1, g0, g1 = wf[0].astype(F32), wf[1].astype(F32), wg[0].astype(F32), wg[1].astype(F32)
    swg[...] = (
        jnp.sum(f0 * uf0 + f1 * uf1 + g0 * ug0 + g1 * ug1, axis=0, keepdims=True)
        + rows[102:103]
    )
    dsb[...] = jnp.sum((f0 + f1) * fb + (g0 + g1) * gb, axis=0, keepdims=True) + mb
    dskip[:, 0:TILE] = v[C : 2 * C]
    dskip[:, TILE:] = v[2 * C : 3 * C]
    dskipb[:, 0:TILE] = v[3 * C : 3 * C + 1]
    dskipb[:, TILE:] = v[3 * C + 1 : 3 * C + 2]


def neighbour(value, steps):
    count = lax.axis_size("seg")
    pairs = [(i, i + steps) for i in range(max(0, -steps), min(count, count - steps))]
    return lax.ppermute(value, "seg", pairs)


def seg_ring(value, shift):
    return lax.ppermute(value, "seg", [(i, shift(i)) for i in range(lax.axis_size("seg"))])


def whole(shape):
    return pl.BlockSpec(shape, lambda *_: (0,) * len(shape))


def params(**kw):
    return pltpu.CompilerParams(vmem_limit_bytes=VMEM_LIMIT, **kw)


VMEM = pl.BlockSpec(memory_space=pltpu.VMEM)
ANY = pl.BlockSpec(memory_space=pl.ANY)
HBM = pl.BlockSpec(memory_space=pltpu.HBM)


def forward_call(base, count, xs, coef, mix, bandt, zown, before):
    more = [] if before is None else [before]
    return pl.pallas_call(
        functools.partial(forward_kernel, base, count),
        grid=(count,),
        out_shape=jax.ShapeDtypeStruct((BR * TOUT * C, W), BF16),
        in_specs=[VMEM] * 4
        + [pl.BlockSpec((ROWS, W), lambda i: (i + base % 4, 0))]
        + [ANY] * len(more),
        out_specs=pl.BlockSpec((ROWS, W), lambda i: (i + base, 0)),
        scratch_shapes=[
            pltpu.VMEM((ROWS, 2 * W), BF16),
            pltpu.VMEM((ROWS, 3 * W), BF16),
            pltpu.VMEM((ROWS, 2 * W), BF16),
            pltpu.VMEM((3 * ROWS, W), BF16),
        ],
        input_output_aliases={5: 0} if more else {},
        compiler_params=params(),
        name="forward",
    )(xs, coef, mix, bandt, zown, *more)


def backward_call(sample, xs, coef, mixt, wsk, wskt, bsk, band, gl, go, gr, gs, before):
    more = [] if before is None else [before]
    slab = pl.BlockSpec((ROWS, W), lambda i: (i, 0))
    own = pl.BlockSpec((ROWS, W), lambda i: (i + 4 * sample, 0))
    per_sample = pl.BlockSpec((1, SKIP, W), lambda i: (sample, 0, 0))
    return pl.pallas_call(
        functools.partial(backward_kernel, sample),
        grid=(4,),
        out_shape=(
            jax.ShapeDtypeStruct((BR, SKIP, W), BF16),
            jax.ShapeDtypeStruct((PAY, TILE), F32),
            jax.ShapeDtypeStruct((TOUT * C, W), BF16),
        ),
        in_specs=[VMEM] * 7 + [slab, own, slab, per_sample] + [ANY] * len(more),
        out_specs=(per_sample, whole((PAY, TILE)), slab),
        scratch_shapes=[
            pltpu.VMEM((ROWS, 3 * W), BF16),
            pltpu.VMEM((ROWS, 2 * W), BF16),
            pltpu.VMEM((3 * ROWS, W), BF16),
            pltpu.VMEM((ROWS, W), F32),
            pltpu.VMEM((ROWS, W), F32),
            pltpu.VMEM((ROWS, W), F32),
            pltpu.VMEM((8, C, TILE), F32),
            pltpu.VMEM((3 * ROWS, ROWS), F32),
            pltpu.VMEM((C + 16, SKIP), F32),
            pltpu.VMEM((C, W), F32),
        ],
        input_output_aliases={11: 0} if more else {},
        compiler_params=params(),
        name="backward",
    )(xs, coef, mixt, wsk, wskt, bsk, band, gl, go, gr, gs, *more)


def send(speeds, cols, grad):
    half = pltpu.HBM((grad.shape[0] // 2, W), BF16)
    return pl.pallas_call(
        message_kernel,
        out_shape=(jax.ShapeDtypeStruct((32, 4, 3 * W), BF16), half, half),
        in_specs=[HBM] * 3,
        out_specs=(VMEM, HBM, HBM),
        scratch_shapes=[
            pltpu.SMEM((TILES, 3), jnp.int32),
            pltpu.VMEM((3, 16384), F32),
            pltpu.VMEM((4, 16384 + 2 * W), F32),
            pltpu.VMEM((2, grad.shape[0] // 2, W), BF16),
            pltpu.SemaphoreType.DMA((6,)),
        ],
        compiler_params=params(),
        name="message",
    )(*(pltpu.with_memory_space_constraint(a, pltpu.HBM) for a in (cols, speeds, grad)))


def prepare(msg, vals, w_start, b_start, w_filter, b_filter, w_gate, b_gate, w_mix, b_mix, w_skip, b_skip):
    row = lambda a: a.reshape(1, -1)
    small = [
        row(w_start), row(b_start), w_filter, row(b_filter), w_gate, row(b_gate), w_mix, row(b_mix),
        w_skip.T, row(b_skip), *vals,
    ]
    return pl.pallas_call(
        prep_kernel,
        grid=(1,),
        out_shape=(
            jax.ShapeDtypeStruct((9 * C, TILE), F32),
            jax.ShapeDtypeStruct((ROWS, 3 * ROWS), BF16),
            jax.ShapeDtypeStruct((ROWS, 3 * ROWS), BF16),
            jax.ShapeDtypeStruct((SKIP, C), BF16),
            jax.ShapeDtypeStruct((SKIP, TILE), F32),
            jax.ShapeDtypeStruct((4, 3 * PAIR, PAIR), BF16),
            jax.ShapeDtypeStruct((4, 3 * PAIR, PAIR), BF16),
            jax.ShapeDtypeStruct((BR * T_IN, 3 * W), F32),
        ),
        in_specs=[whole(a.shape) for a in small] + [VMEM],
        out_specs=(VMEM,) * 8,
        compiler_params=params(),
        name="prep",
    )(*small, msg)


def body(
    speeds, w_start, b_start, w_filter, b_filter, w_gate, b_gate, adj_cols, adj_vals,
    w_mix, b_mix, w_skip, b_skip, grad_res, grad_skip,
):
    barrier = lax.optimization_barrier
    half = TOUT * C
    grad = grad_res.reshape(BR * half, W)
    msg, first, second = send(speeds, adj_cols, grad)
    halo0 = neighbour(first, 1), neighbour(first, -1)
    msg, vals = barrier((msg, adj_vals))
    msg = lax.all_to_all(msg, "seg", split_axis=0, concat_axis=0, tiled=True)
    vals = (neighbour(vals, 1), adj_vals, neighbour(vals, -1))
    coef, mix, mixt, wsk, bsk, band, bandt, xs = prepare(
        msg, vals, w_start, b_start, w_filter, b_filter, w_gate, b_gate, w_mix, b_mix, w_skip, b_skip
    )
    xs, second = barrier((xs, second))
    halo1 = neighbour(second, 1), neighbour(second, -1)

    common = (coef, mixt, wsk, w_skip.T, bsk, band)
    skip, pay0, z0 = backward_call(0, xs, *common, halo0[0], grad, halo0[1], grad_skip, None)
    pay0, xs = barrier((pay0, xs))
    res = forward_call(0, 4, xs, coef, mix, bandt, z0, None)
    res, xs = barrier((res, xs))
    skip, pay1, z1 = backward_call(1, xs, *common, halo1[0], grad, halo1[1], grad_skip, skip)

    v = pay0 + pay1
    v = v + seg_ring(v, lambda i: i ^ 1)

    def forward(base, count, v, before):
        v, z_now = barrier((v, z1))
        return v, forward_call(base, count, xs, coef, mix, bandt, z_now, before)

    v, res = forward(4, 2, v, res)
    v = v + sum(seg_ring(v, lambda i, k=k: (i // 8) * 8 + ((i // 2 + k) % 4) * 2 + i % 2) for k in (1, 2, 3))
    v, res = barrier((v, res))
    v, res = forward(6, 1, v, res)
    v = v + sum(seg_ring(v, lambda i, k=k: (i + 8 * k) % 32) for k in (1, 2, 3))
    v, res = barrier((v, res))
    v, res = forward(7, 1, v, res)
    others = [lax.ppermute(v, "rep", [(i, (i + k) % 4) for i in range(4)]) for k in (1, 2, 3)]

    row = jax.ShapeDtypeStruct((1, C), F32)
    taps = jax.ShapeDtypeStruct((2, C, C), F32)
    small = (v, *others, w_start.reshape(1, C), b_start.reshape(1, C), w_filter, w_gate)
    swg, dsb, dfil, dfb, dgat, dgb, dmix, dmixb, dskip, dskipb = pl.pallas_call(
        finish_kernel,
        grid=(1,),
        out_shape=(
            row, row, taps, row, taps, row, jax.ShapeDtypeStruct((C, 3 * C), F32), row,
            jax.ShapeDtypeStruct((C, SKIP), F32), jax.ShapeDtypeStruct((1, SKIP), F32),
        ),
        in_specs=[whole(a.shape) for a in small],
        out_specs=(whole((1, C)), whole((1, C)), whole((2, C, C)), whole((1, C)), whole((2, C, C)),
                   whole((1, C)), whole((C, 3 * C)), whole((1, C)), whole((C, SKIP)), whole((1, SKIP))),
        compiler_params=params(),
        name="finish",
    )(*small)
    vec = lambda a: a.reshape(-1)
    return (
        res.reshape(BR, TOUT, C, W), skip, vec(swg), vec(dsb), dfil, vec(dfb), dgat, vec(dgb),
        dmix, vec(dmixb), dskip.T, vec(dskipb),
    )


def solution(mesh):
    placed = (
        P(("rep", "seg"), None), P(), P(), P(), P(), P(), P(), P("seg", None),
        P("seg", None, None, None), P(), P(), P(), P(), P("rep", None, None, "seg"),
        P("rep", None, "seg"),
    )
    return jax.shard_map(
        body,
        mesh=mesh,
        in_specs=placed,
        out_specs=(P("rep", None, None, "seg"), P("rep", None, "seg")) + (P(),) * 10,
        check_vma=False,
    )
```

```python
import functools
import math

import jax
import jax.numpy as jnp
from jax import lax
from jax.experimental import pallas as pl
from jax.experimental.pallas import tpu as pltpu
from jax.sharding import PartitionSpec as P

C = 32
SKIP = 256
TILE = 128
DIL = 16
TOUT = 32
T_IN = 48
BR = 2
TILES = 4
W = TILES * TILE
PAIR = 2 * TILE
TG = 8
ROWS = TG * C
F32 = jnp.float32
BF16 = jnp.bfloat16
A0F, A1F, CF, A0G, A1G, CG, WS, BS, BM = range(9)
PAY = 104
RES_SCALE = 1.0 / math.sqrt(8 * TOUT * 16384)
SKIP_SCALE = 1.0 / math.sqrt(8 * 16384)
VMEM_LIMIT = 20 * 1024 * 1024


def dot(a, b):
    return jnp.dot(a, b, preferred_element_type=F32)


def dot_nt(a, b):
    return lax.dot_general(a, b, (((1,), (1,)), ((), ())), preferred_element_type=F32)


def column(row):
    n = row.shape[1]
    r = lax.broadcasted_iota(jnp.int32, (n, n), 0)
    c = lax.broadcasted_iota(jnp.int32, (n, n), 1)
    return jnp.sum(jnp.where(r == c, jnp.broadcast_to(row, (n, n)), 0.0), axis=1, keepdims=True)


def block_diag(w):
    row = jnp.concatenate([w] * TG, axis=1)
    full = jnp.concatenate([row] * TG, axis=0)
    r = lax.broadcasted_iota(jnp.int32, (ROWS, ROWS), 0) // C
    c = lax.broadcasted_iota(jnp.int32, (ROWS, ROWS), 1) // C
    return jnp.where(r == c, full, 0.0)


def message_kernel(cols_hbm, speeds, msg, cols, rows, wide, sems):
    loads = [
        pltpu.make_async_copy(speeds, rows, sems.at[0]),
        pltpu.make_async_copy(cols_hbm, cols, sems.at[1]),
    ]
    for copy in loads:
        copy.start()
    wide[:, 0:W] = jnp.zeros((4, W), F32)
    wide[:, W + 16384 :] = jnp.zeros((4, W), F32)
    loads[0].wait()
    loads[1].wait()
    wide[0:3, W : W + 16384] = rows[...]
    base = lax.axis_index("seg") * TILES
    offsets = jnp.concatenate(
        [
            jnp.broadcast_to((cols[t, k] - (base + t)).astype(F32), (4, TILE))
            for t in range(TILES)
            for k in range(3)
        ],
        axis=1,
    )
    row = lax.broadcasted_iota(jnp.int32, (4, 3 * W), 0)
    for d in range(32):
        msg[d] = jnp.where(row == 3, offsets, wide[:, d * W : (d + 3) * W]).astype(BF16)


def prep_kernel(
    ws, bs, wf, bf, wg, bg, wm, bm, wskt, bsk, vl, vo, vr, msg,
    coef, mix, mixt, wsk, bskc, band, bandt, xs,
):
    wrow, brow = ws[...], bs[...]

    def put(i, col):
        coef[i * C : (i + 1) * C, :] = jnp.broadcast_to(col, (C, TILE))

    def lane_sum(m):
        return jnp.sum(m, axis=1, keepdims=True)

    for w, bias, base, scale in ((wf, bf, A0F, 1.0), (wg, bg, A0G, 0.5)):
        w0, w1 = w[0].astype(F32), w[1].astype(F32)
        put(base, lane_sum(w0 * wrow) * scale)
        put(base + 1, lane_sum(w1 * wrow) * scale)
        put(base + 2, (lane_sum((w0 + w1) * brow) + column(bias[...])) * scale)
    put(WS, column(wrow))
    put(BS, column(brow))
    put(BM, column(bm[...]))
    for h in range(3):
        w = wm[:, h * C : (h + 1) * C].astype(F32)
        mix[:, h * ROWS : (h + 1) * ROWS] = block_diag(w * 0.5).astype(BF16)
        mixt[:, h * ROWS : (h + 1) * ROWS] = block_diag(w.T).astype(BF16)
    wsk[...] = (wskt[...].astype(F32) * 0.5).T.astype(BF16)
    bskc[...] = jnp.broadcast_to(column(bsk[...]), (SKIP, TILE))

    for i in range(32):
        xs[3 * i : 3 * i + 3, :] = msg[i].astype(F32)[0:3]

    def store(dst, row, col, v):
        j = col // 2 - 1
        at = row - 2 * j
        if 0 <= j < 4 and 0 <= at < 6:
            dst[j, at * TILE : (at + 1) * TILE, (col % 2) * TILE : (col % 2 + 1) * TILE] = v

    zero = jnp.zeros((TILE, TILE), BF16)
    for dst in (band, bandt):
        for j in range(4):
            dst[j, 0:TILE, TILE:] = zero
            dst[j, 5 * TILE :, 0:TILE] = zero
    seg = lax.axis_index("seg")
    for src, vals in enumerate((vl, vo, vr)):
        sender = jnp.clip(seg + src - 1, 0, 31)
        for t in range(TILES):
            m = src * TILES + t
            v0, v1, v2 = (vals[t, k] for k in range(3))
            u0, u1, u2 = v0.T, v1.T, v2.T

            def off(k, t=t, sender=sender):
                return msg[sender, :, (t * 3 + k) * TILE : (t * 3 + k + 1) * TILE].astype(F32)[3:4]

            o1, o2 = off(1), off(2)
            store(band, m, m, v0)
            store(bandt, m, m, u0)
            for o in (-2, -1, 1, 2):
                q = m + o
                if not 0 <= q < 12:
                    continue
                c2 = jnp.broadcast_to(jnp.where(o2 == o, 1.0, 0.0).astype(BF16), (TILE, TILE))
                v, u = c2 * v2, c2 * u2
                if abs(o) == 2:
                    c1 = jnp.broadcast_to(jnp.where(o1 == o, 1.0, 0.0).astype(BF16), (TILE, TILE))
                    v, u = v + c1 * v1, u + c1 * u1
                store(band, m, q, v)
                store(bandt, q, m, u)


def hops(ext, one, band, put, between):
    for p in range(4):
        one[:, p * PAIR : (p + 1) * PAIR] = dot(
            ext[:, p * PAIR : (p + 3) * PAIR], band[p]
        ).astype(BF16)
        between()
    for p in range(2):
        put(p, dot(one[:, p * PAIR : (p + 3) * PAIR], band[p + 1]).astype(BF16))
        between()


def coefs(coef, *which):
    return [coef[i * C : (i + 1) * C, :] for i in which]


def spread(bodies, slots):
    queue = list(bodies)
    share = -(-len(queue) // slots)

    def emit():
        for _ in range(min(share, len(queue))):
            queue.pop(0)()

    return emit


def lane_tile(t):
    return slice(t * TILE, (t + 1) * TILE)


def slab_rows(k):
    return slice(k * C, (k + 1) * C)


def gates(coef, p, q):
    a0f, a1f, cf, a0g, a1g, cg = coefs(coef, A0F, A1F, CF, A0G, A1G, CG)
    return jnp.tanh(a0f * p + a1f * q + cf), jnp.tanh(a0g * p + a1g * q + cg) + 1.0


def forward_kernel(
    xs, coef, mix, bandt, wsk, bsk, wskt, grad, gskip,
    res, skip, z, dfil, dgat, esum, dsk, extra, ahead, zext, one, stack,
):
    i = pl.program_id(0)

    def at(step):
        row = ((step // 4) * 6 + step % 4) * TG
        return (
            xs.at[pl.ds(pl.multiple_of(row, TG), TG)],
            xs.at[pl.ds(pl.multiple_of(row + DIL, TG), TG)],
        )

    def look_ahead(step, k, t):
        x0, x1 = at(step)

        def emit():
            lanes = lane_tile(t)
            f, u = gates(coef, x0[k : k + 1, lanes], x1[k : k + 1, lanes])
            fu = f * u
            ahead[slab_rows(k), lanes] = fu.astype(BF16)
            if 4 <= t < 8:
                rows = pl.ds(pl.multiple_of(step * ROWS + k * C, C), C)
                dfil[rows, lane_tile(t - 4)] = (u - f * fu).astype(BF16)
                dgat[rows, lane_tile(t - 4)] = (fu * (2.0 - u)).astype(BF16)

        return emit

    @pl.when(i == 0)
    def _():
        esum[...] = jnp.zeros_like(esum)
        dsk[...] = jnp.zeros_like(dsk)
        for k in range(TG):
            for t in range(12):
                look_ahead(i, k, t)()

    mine = pl.ds(pl.multiple_of(i * ROWS, ROWS), ROWS)
    zext[...] = ahead[...]
    stack[0:ROWS, :] = ahead[:, W : 2 * W]
    z[mine, :] = ahead[:, W : 2 * W]
    ahead_step = jnp.minimum(i + 1, 7)
    emit = spread([look_ahead(ahead_step, k, t) for k in range(TG) for t in range(12)], 6)

    def put(p, v):
        stack[2 * ROWS : 3 * ROWS, p * PAIR : (p + 1) * PAIR] = v

    hops(zext, one, bandt, put, emit)
    stack[ROWS : 2 * ROWS, :] = one[:, PAIR : PAIR + W]
    mixed = dot(mix[...], stack[...])
    ws, bs, bm = coefs(coef, WS, BS, BM)
    bb = bs + bm
    x1 = at(i)[1]
    go = grad.at[mine]
    se, sq = esum[0], esum[1]
    for k in range(TG):
        for t in range(TILES):
            q = x1[k : k + 1, W + t * TILE : W + (t + 1) * TILE]
            r, lanes = slab_rows(k), lane_tile(t)
            res[r, lanes] = (mixed[r, lanes] + (ws * q + bb)).astype(BF16)
            e = go[r, lanes].astype(F32)
            se = se + e
            sq = sq + e * q
    esum[0] = se
    esum[1] = sq

    @pl.when(i % 4 == 3)
    def _():
        gs = gskip.at[i // 4]
        bias = jnp.concatenate([bsk[...]] * TILES, axis=1)
        z31 = stack[ROWS - C : ROWS, :]
        twos = jnp.full((16, W), 2.0, BF16)
        skip[0] = (dot(wsk[...], z31) + bias).astype(BF16)
        dsk[...] += dot_nt(jnp.concatenate([z31, twos], axis=0), gs[...])
        extra[i // 4] = dot(wskt[...], gs[...]) * (SKIP_SCALE / RES_SCALE)


def backward_kernel(
    xs, mixt, band, gl, grad, gr, z, dfil, dgat, esum, dsk, extra,
    pay, ext, one, stack, dzs, acc, dmx,
):
    i = pl.program_id(0)
    mine = pl.ds(pl.multiple_of(i * ROWS, ROWS), ROWS)
    go, zb, fa, ga = (ref.at[mine] for ref in (grad, z, dfil, dgat))
    at = ((i // 4) * 6 + i % 4) * TG
    x0 = xs.at[pl.ds(pl.multiple_of(at, TG), TG)]
    x1 = xs.at[pl.ds(pl.multiple_of(at + DIL, TG), TG)]

    @pl.when(i == 0)
    def _():
        acc[...] = jnp.zeros_like(acc)
        dmx[...] = jnp.zeros_like(dmx)

    ext[:, 0:W] = gl[...]
    ext[:, W : 2 * W] = go[...]
    ext[:, 2 * W : 3 * W] = gr[...]
    stack[0:ROWS, :] = go[...]

    def put(p, v):
        stack[2 * ROWS : 3 * ROWS, p * PAIR : (p + 1) * PAIR] = v

    hops(ext, one, band, put, lambda: None)
    stack[ROWS : 2 * ROWS, :] = one[:, PAIR : PAIR + W]
    dzs[...] = dot(mixt[...], stack[...])
    dzs[ROWS - C : ROWS, :] += extra[i // 4] * jnp.where(i % 4 == 3, 1.0, 0.0)

    sums = [acc[j] for j in range(6)]

    def local(k, t):
        def emit():
            r, lanes = slab_rows(k), lane_tile(t)
            across = slice(W + t * TILE, W + (t + 1) * TILE)
            p, q = x0[k : k + 1, across], x1[k : k + 1, across]
            dz = dzs[r, lanes]
            df = dz * fa[r, lanes].astype(F32)
            dgt = dz * ga[r, lanes].astype(F32)
            for j, term in enumerate((df * p, df * q, df, dgt * p, dgt * q, dgt)):
                sums[j] = sums[j] + term

        return emit

    emit = spread([local(k, t) for k in range(TG) for t in range(TILES)], 3)
    for h in range(3):
        part = slice(h * ROWS, (h + 1) * ROWS)
        dmx[part, :] += dot_nt(stack[part, :], zb[...])
        emit()
    for j in range(6):
        acc[j] = sums[j]

    @pl.when(i == 7)
    def _():
        r = lax.broadcasted_iota(jnp.int32, (ROWS, ROWS), 0) // C
        c = lax.broadcasted_iota(jnp.int32, (ROWS, ROWS), 1) // C
        lane = lax.broadcasted_iota(jnp.int32, (C, TILE), 1)
        packed = jnp.zeros((C, TILE), F32)
        for h in range(3):
            m = jnp.where(r == c, dmx[h * ROWS : (h + 1) * ROWS, :], 0.0)
            v = m[0:C]
            for k in range(1, TG):
                v = v + m[k * C : (k + 1) * C]
            v = v[:, :TILE] + v[:, TILE:]
            v = v + pltpu.roll(v, 64, 1)
            v = v + pltpu.roll(v, 32, 1)
            packed = jnp.where(lane // C == h, v, packed)
        packed = packed * (0.5 * RES_SCALE)
        parts = [(acc[j], 0.5 if j < 3 else 0.25) for j in range(6)] + [(esum[1], 1.0), (esum[0], 1.0)]
        for j, (a, scale) in enumerate(parts):
            s = jnp.sum(a, axis=1, keepdims=True) * (scale * RES_SCALE)
            packed = jnp.where(lane == 96 + j, s, packed)
        pay[0:C, :] = packed
        pay[C : 2 * C, :] = dsk[0:C, 0:TILE] * (0.5 * SKIP_SCALE)
        pay[2 * C : 3 * C, :] = dsk[0:C, TILE:] * (0.5 * SKIP_SCALE)
        sub = lax.broadcasted_iota(jnp.int32, (8, TILE), 0)
        pay[3 * C : PAY, :] = jnp.where(
            sub == 0, dsk[C : C + 8, 0:TILE], dsk[C : C + 8, TILE:]
        ) * (0.5 * SKIP_SCALE)


def finish_kernel(
    p0, p1, p2, p3, ws, bs, wf, wg,
    swg, dsb, dfil, dfb, dgat, dgb, dmix, dmixb, dskip, dskipb,
):
    v = (p0[...] + p1[...]) + (p2[...] + p3[...])
    wrow, brow = ws[...], bs[...]
    head = v[0:C]
    rows = head.T
    uf0, uf1, fb, ug0, ug1, gb = (head[:, 96 + j : 97 + j] for j in range(6))
    dmix[...] = head[:, 0:96]
    dfil[0] = uf0 * wrow + fb * brow
    dfil[1] = uf1 * wrow + fb * brow
    dgat[0] = ug0 * wrow + gb * brow
    dgat[1] = ug1 * wrow + gb * brow
    dfb[...] = rows[98:99]
    dgb[...] = rows[101:102]
    mb = rows[103:104]
    dmixb[...] = mb
    f0, f1, g0, g1 = wf[0].astype(F32), wf[1].astype(F32), wg[0].astype(F32), wg[1].astype(F32)
    swg[...] = (
        jnp.sum(f0 * uf0 + f1 * uf1 + g0 * ug0 + g1 * ug1, axis=0, keepdims=True)
        + rows[102:103]
    )
    dsb[...] = jnp.sum((f0 + f1) * fb + (g0 + g1) * gb, axis=0, keepdims=True) + mb
    dskip[:, 0:TILE] = v[C : 2 * C]
    dskip[:, TILE:] = v[2 * C : 3 * C]
    dskipb[:, 0:TILE] = v[3 * C : 3 * C + 1]
    dskipb[:, TILE:] = v[3 * C + 1 : 3 * C + 2]


def neighbour(value, steps):
    count = lax.axis_size("seg")
    pairs = [(i, i + steps) for i in range(max(0, -steps), min(count, count - steps))]
    return lax.ppermute(value, "seg", pairs)


def seg_ring(value, shift):
    return lax.ppermute(value, "seg", [(i, shift(i)) for i in range(lax.axis_size("seg"))])


def whole(shape):
    return pl.BlockSpec(shape, lambda *_: (0,) * len(shape))


def params(**kw):
    return pltpu.CompilerParams(vmem_limit_bytes=VMEM_LIMIT, **kw)


VMEM = pl.BlockSpec(memory_space=pltpu.VMEM)
ANY = pl.BlockSpec(memory_space=pl.ANY)
HBM = pl.BlockSpec(memory_space=pltpu.HBM)


def forward_call(xs, coef, mix, bandt, wsk, bsk, wskt, grad, gskip):
    rows = BR * TOUT * C
    return pl.pallas_call(
        forward_kernel,
        grid=(8,),
        out_shape=(
            jax.ShapeDtypeStruct((rows, W), BF16),
            jax.ShapeDtypeStruct((BR, SKIP, W), BF16),
            jax.ShapeDtypeStruct((rows, W), BF16),
            jax.ShapeDtypeStruct((rows, W), BF16),
            jax.ShapeDtypeStruct((rows, W), BF16),
            jax.ShapeDtypeStruct((2, C, TILE), F32),
            jax.ShapeDtypeStruct((C + 16, SKIP), F32),
            jax.ShapeDtypeStruct((BR, C, W), F32),
        ),
        in_specs=[VMEM] * 9,
        out_specs=(
            pl.BlockSpec((ROWS, W), lambda i: (i, 0)),
            pl.BlockSpec((1, SKIP, W), lambda i: (i // 4, 0, 0)),
        )
        + (VMEM,) * 6,
        scratch_shapes=[
            pltpu.VMEM((ROWS, 3 * W), BF16),
            pltpu.VMEM((ROWS, 3 * W), BF16),
            pltpu.VMEM((ROWS, 2 * W), BF16),
            pltpu.VMEM((3 * ROWS, W), BF16),
        ],
        compiler_params=params(),
        cost_estimate=pl.CostEstimate(
            flops=20_000_000_000, bytes_accessed=16_000_000, transcendentals=6_000_000
        ),
        name="forward",
    )(xs, coef, mix, bandt, wsk, bsk, wskt, grad, gskip)


def backward_call(xs, mixt, band, gl, go, gr, *early):
    slab = pl.BlockSpec((ROWS, W), lambda i: (i, 0))
    return pl.pallas_call(
        backward_kernel,
        grid=(8,),
        out_shape=jax.ShapeDtypeStruct((PAY, TILE), F32),
        in_specs=[VMEM] * 3 + [slab, VMEM, slab] + [VMEM] * 6,
        out_specs=VMEM,
        scratch_shapes=[
            pltpu.VMEM((ROWS, 3 * W), BF16),
            pltpu.VMEM((ROWS, 2 * W), BF16),
            pltpu.VMEM((3 * ROWS, W), BF16),
            pltpu.VMEM((ROWS, W), F32),
            pltpu.VMEM((6, C, TILE), F32),
            pltpu.VMEM((3 * ROWS, ROWS), F32),
        ],
        compiler_params=params(),
        name="backward",
    )(xs, mixt, band, gl, go, gr, *early)


def in_hbm(a):
    return pltpu.with_memory_space_constraint(a, pltpu.HBM)


def send(speeds, cols):
    return pl.pallas_call(
        message_kernel,
        out_shape=jax.ShapeDtypeStruct((32, 4, 3 * W), BF16),
        in_specs=[HBM] * 2,
        out_specs=VMEM,
        scratch_shapes=[
            pltpu.SMEM((TILES, 3), jnp.int32),
            pltpu.VMEM((3, 16384), F32),
            pltpu.VMEM((4, 16384 + 2 * W), F32),
            pltpu.SemaphoreType.DMA((2,)),
        ],
        compiler_params=params(),
        name="message",
    )(in_hbm(cols), in_hbm(speeds))


def prepare(msg, vals, w_start, b_start, w_filter, b_filter, w_gate, b_gate, w_mix, b_mix, w_skip, b_skip):
    row = lambda a: a.reshape(1, -1)
    small = [
        row(w_start), row(b_start), w_filter, row(b_filter), w_gate, row(b_gate), w_mix, row(b_mix),
        w_skip.T, row(b_skip), *vals,
    ]
    return pl.pallas_call(
        prep_kernel,
        grid=(1,),
        out_shape=(
            jax.ShapeDtypeStruct((9 * C, TILE), F32),
            jax.ShapeDtypeStruct((ROWS, 3 * ROWS), BF16),
            jax.ShapeDtypeStruct((ROWS, 3 * ROWS), BF16),
            jax.ShapeDtypeStruct((SKIP, C), BF16),
            jax.ShapeDtypeStruct((SKIP, TILE), F32),
            jax.ShapeDtypeStruct((4, 3 * PAIR, PAIR), BF16),
            jax.ShapeDtypeStruct((4, 3 * PAIR, PAIR), BF16),
            jax.ShapeDtypeStruct((BR * T_IN, 3 * W), F32),
        ),
        in_specs=[whole(a.shape) for a in small] + [VMEM],
        out_specs=(VMEM,) * 8,
        compiler_params=params(),
        name="prep",
    )(*(in_hbm(a) for a in small), msg)


def body(
    speeds, w_start, b_start, w_filter, b_filter, w_gate, b_gate, adj_cols, adj_vals,
    w_mix, b_mix, w_skip, b_skip, grad_res, grad_skip,
):
    barrier = lax.optimization_barrier
    grad = grad_res.reshape(BR * TOUT * C, W)
    msg = send(speeds, adj_cols)
    msg, vals = barrier((msg, adj_vals))
    msg = lax.all_to_all(msg, "seg", split_axis=0, concat_axis=0, tiled=True)
    vals = (neighbour(vals, 1), adj_vals, neighbour(vals, -1))
    *vals, grad_now = barrier((*vals, grad))
    grad_l, grad_r = neighbour(grad_now, 1), neighbour(grad_now, -1)
    coef, mix, mixt, wsk, bsk, band, bandt, xs = prepare(
        msg, vals, w_start, b_start, w_filter, b_filter, w_gate, b_gate, w_mix, b_mix, w_skip, b_skip
    )
    res, skip, *early = forward_call(xs, coef, mix, bandt, wsk, bsk, w_skip.T, grad, grad_skip)
    v = backward_call(xs, mixt, band, grad_l, grad, grad_r, *early)

    v = v + seg_ring(v, lambda i: i ^ 1)
    v = v + sum(seg_ring(v, lambda i, k=k: (i // 8) * 8 + ((i // 2 + k) % 4) * 2 + i % 2) for k in (1, 2, 3))
    v = v + sum(seg_ring(v, lambda i, k=k: (i + 8 * k) % 32) for k in (1, 2, 3))
    others = [lax.ppermute(v, "rep", [(i, (i + k) % 4) for i in range(4)]) for k in (1, 2, 3)]

    row = jax.ShapeDtypeStruct((1, C), F32)
    taps = jax.ShapeDtypeStruct((2, C, C), F32)
    small = (v, *others, w_start.reshape(1, C), b_start.reshape(1, C), w_filter, w_gate)
    swg, dsb, dfil, dfb, dgat, dgb, dmix, dmixb, dskip, dskipb = pl.pallas_call(
        finish_kernel,
        grid=(1,),
        out_shape=(
            row, row, taps, row, taps, row, jax.ShapeDtypeStruct((C, 3 * C), F32), row,
            jax.ShapeDtypeStruct((C, SKIP), F32), jax.ShapeDtypeStruct((1, SKIP), F32),
        ),
        in_specs=[whole(a.shape) for a in small],
        out_specs=(whole((1, C)), whole((1, C)), whole((2, C, C)), whole((1, C)), whole((2, C, C)),
                   whole((1, C)), whole((C, 3 * C)), whole((1, C)), whole((C, SKIP)), whole((1, SKIP))),
        compiler_params=params(),
        name="finish",
    )(*small)
    vec = lambda a: a.reshape(-1)
    return (
        res.reshape(BR, TOUT, C, W), skip, vec(swg), vec(dsb), dfil, vec(dfb), dgat, vec(dgb),
        dmix, vec(dmixb), dskip.T, vec(dskipb),
    )


def solution(mesh):
    placed = (
        P(("rep", "seg"), None), P(), P(), P(), P(), P(), P(), P("seg", None),
        P("seg", None, None, None), P(), P(), P(), P(), P("rep", None, None, "seg"),
        P("rep", None, "seg"),
    )
    return jax.shard_map(
        body,
        mesh=mesh,
        in_specs=placed,
        out_specs=(P("rep", None, None, "seg"), P("rep", None, "seg")) + (P(),) * 10,
        check_vma=False,
    )
```

```python
import functools
import math

import jax
import jax.numpy as jnp
from jax import lax
from jax.experimental import pallas as pl
from jax.experimental.pallas import tpu as pltpu
from jax.sharding import PartitionSpec as P

C = 32
SKIP = 256
TILE = 128
DIL = 16
TOUT = 32
T_IN = 48
BR = 2
TILES = 4
W = TILES * TILE
PAIR = 2 * TILE
TG = 8
ROWS = TG * C
F32 = jnp.float32
BF16 = jnp.bfloat16
A0F, A1F, CF, A0G, A1G, CG, WS, BS, BM = range(9)
PAY = 104
RES_SCALE = 1.0 / math.sqrt(8 * TOUT * 16384)
SKIP_SCALE = 1.0 / math.sqrt(8 * 16384)
VMEM_LIMIT = 20 * 1024 * 1024


def dot(a, b):
    return jnp.dot(a, b, preferred_element_type=F32)


def dot_nt(a, b):
    return lax.dot_general(a, b, (((1,), (1,)), ((), ())), preferred_element_type=F32)


def column(row):
    n = row.shape[1]
    r = lax.broadcasted_iota(jnp.int32, (n, n), 0)
    c = lax.broadcasted_iota(jnp.int32, (n, n), 1)
    return jnp.sum(jnp.where(r == c, jnp.broadcast_to(row, (n, n)), 0.0), axis=1, keepdims=True)


def block_diag(w):
    row = jnp.concatenate([w] * TG, axis=1)
    full = jnp.concatenate([row] * TG, axis=0)
    r = lax.broadcasted_iota(jnp.int32, (ROWS, ROWS), 0) // C
    c = lax.broadcasted_iota(jnp.int32, (ROWS, ROWS), 1) // C
    return jnp.where(r == c, full, 0.0)


def message_kernel(cols_hbm, speeds, msg, cols, rows, wide, sems):
    loads = [
        pltpu.make_async_copy(speeds, rows, sems.at[0]),
        pltpu.make_async_copy(cols_hbm, cols, sems.at[1]),
    ]
    for copy in loads:
        copy.start()
    wide[:, 0:W] = jnp.zeros((4, W), F32)
    wide[:, W + 16384 :] = jnp.zeros((4, W), F32)
    loads[0].wait()
    loads[1].wait()
    wide[0:3, W : W + 16384] = rows[...]
    base = lax.axis_index("seg") * TILES
    offsets = jnp.concatenate(
        [
            jnp.broadcast_to((cols[t, k] - (base + t)).astype(F32), (4, TILE))
            for t in range(TILES)
            for k in range(3)
        ],
        axis=1,
    )
    row = lax.broadcasted_iota(jnp.int32, (4, 3 * W), 0)
    for d in range(32):
        msg[d] = jnp.where(row == 3, offsets, wide[:, d * W : (d + 3) * W]).astype(BF16)


def prep_kernel(
    ws, bs, wf, bf, wg, bg, wm, bm, wskt, bsk, vl, vo, vr, msg,
    coef, mix, mixt, wsk, bskc, band, bandt, xs,
):
    wrow, brow = ws[...], bs[...]

    def put(i, col):
        coef[i * C : (i + 1) * C, :] = jnp.broadcast_to(col, (C, TILE))

    def lane_sum(m):
        return jnp.sum(m, axis=1, keepdims=True)

    for w, bias, base, scale in ((wf, bf, A0F, 1.0), (wg, bg, A0G, 0.5)):
        w0, w1 = w[0].astype(F32), w[1].astype(F32)
        put(base, lane_sum(w0 * wrow) * scale)
        put(base + 1, lane_sum(w1 * wrow) * scale)
        put(base + 2, (lane_sum((w0 + w1) * brow) + column(bias[...])) * scale)
    put(WS, column(wrow))
    put(BS, column(brow))
    put(BM, column(bm[...]))
    for h in range(3):
        w = wm[:, h * C : (h + 1) * C].astype(F32)
        mix[:, h * ROWS : (h + 1) * ROWS] = block_diag(w * 0.5).astype(BF16)
        mixt[:, h * ROWS : (h + 1) * ROWS] = block_diag(w.T).astype(BF16)
    wsk[...] = (wskt[...].astype(F32) * 0.5).T.astype(BF16)
    bskc[...] = jnp.broadcast_to(column(bsk[...]), (SKIP, TILE))

    for i in range(32):
        xs[3 * i : 3 * i + 3, :] = msg[i].astype(F32)[0:3]

    def store(dst, row, col, v):
        j = col // 2 - 1
        at = row - 2 * j
        if 0 <= j < 4 and 0 <= at < 6:
            dst[j, at * TILE : (at + 1) * TILE, (col % 2) * TILE : (col % 2 + 1) * TILE] = v

    zero = jnp.zeros((TILE, TILE), BF16)
    for dst in (band, bandt):
        for j in range(4):
            dst[j, 0:TILE, TILE:] = zero
            dst[j, 5 * TILE :, 0:TILE] = zero
    seg = lax.axis_index("seg")
    for src, vals in enumerate((vl, vo, vr)):
        sender = jnp.clip(seg + src - 1, 0, 31)
        for t in range(TILES):
            m = src * TILES + t
            v0, v1, v2 = (vals[t, k] for k in range(3))
            u0, u1, u2 = v0.T, v1.T, v2.T

            def off(k, t=t, sender=sender):
                return msg[sender, :, (t * 3 + k) * TILE : (t * 3 + k + 1) * TILE].astype(F32)[3:4]

            o1, o2 = off(1), off(2)
            store(band, m, m, v0)
            store(bandt, m, m, u0)
            for o in (-2, -1, 1, 2):
                q = m + o
                if not 0 <= q < 12:
                    continue
                c2 = jnp.broadcast_to(jnp.where(o2 == o, 1.0, 0.0).astype(BF16), (TILE, TILE))
                v, u = c2 * v2, c2 * u2
                if abs(o) == 2:
                    c1 = jnp.broadcast_to(jnp.where(o1 == o, 1.0, 0.0).astype(BF16), (TILE, TILE))
                    v, u = v + c1 * v1, u + c1 * u1
                store(band, m, q, v)
                store(bandt, q, m, u)


def hops(ext, one, band, put, between):
    for p in range(4):
        one[:, p * PAIR : (p + 1) * PAIR] = dot(
            ext[:, p * PAIR : (p + 3) * PAIR], band[p]
        ).astype(BF16)
        between()
    for p in range(2):
        put(p, dot(one[:, p * PAIR : (p + 3) * PAIR], band[p + 1]).astype(BF16))
        between()


def coefs(coef, *which):
    return [coef[i * C : (i + 1) * C, :] for i in which]


def spread(bodies, slots):
    queue = list(bodies)
    share = -(-len(queue) // slots)

    def emit():
        for _ in range(min(share, len(queue))):
            queue.pop(0)()

    return emit


def lane_tile(t):
    return slice(t * TILE, (t + 1) * TILE)


def slab_rows(k):
    return slice(k * C, (k + 1) * C)


def gates(coef, p, q):
    a0f, a1f, cf, a0g, a1g, cg = coefs(coef, A0F, A1F, CF, A0G, A1G, CG)
    return jnp.tanh(a0f * p + a1f * q + cf), jnp.tanh(a0g * p + a1g * q + cg) + 1.0


def forward_kernel(
    xs, coef, mix, mixt, band, bandt, wsk, bsk, wskt, grad, gskip,
    res, skip, z, dfil, dgat, e0, g1, esum, dsk, extra, dm0, ahead, zext, one, stack,
):
    i = pl.program_id(0)

    def at(step):
        row = ((step // 4) * 6 + step % 4) * TG
        return (
            xs.at[pl.ds(pl.multiple_of(row, TG), TG)],
            xs.at[pl.ds(pl.multiple_of(row + DIL, TG), TG)],
        )

    def look_ahead(step, k, t):
        x0, x1 = at(step)

        def emit():
            lanes = lane_tile(t)
            f, u = gates(coef, x0[k : k + 1, lanes], x1[k : k + 1, lanes])
            fu = f * u
            ahead[slab_rows(k), lanes] = fu.astype(BF16)
            if 4 <= t < 8:
                rows = pl.ds(pl.multiple_of(step * ROWS + k * C, C), C)
                dfil[rows, lane_tile(t - 4)] = (u - f * fu).astype(BF16)
                dgat[rows, lane_tile(t - 4)] = (fu * (2.0 - u)).astype(BF16)

        return emit

    @pl.when(i == 0)
    def _():
        esum[...] = jnp.zeros_like(esum)
        dsk[...] = jnp.zeros_like(dsk)
        dm0[...] = jnp.zeros_like(dm0)
        for k in range(TG):
            for t in range(12):
                look_ahead(i, k, t)()

    mine = pl.ds(pl.multiple_of(i * ROWS, ROWS), ROWS)
    zext[...] = ahead[...]
    stack[0:ROWS, :] = ahead[:, W : 2 * W]
    z[mine, :] = ahead[:, W : 2 * W]
    ahead_step = jnp.minimum(i + 1, 7)
    emit = spread([look_ahead(ahead_step, k, t) for k in range(TG) for t in range(12)], 6)

    def put(p, v):
        stack[2 * ROWS : 3 * ROWS, p * PAIR : (p + 1) * PAIR] = v

    hops(zext, one, bandt, put, emit)
    stack[ROWS : 2 * ROWS, :] = one[:, PAIR : PAIR + W]
    mixed = dot(mix[...], stack[...])
    ws, bs, bm = coefs(coef, WS, BS, BM)
    bb = bs + bm
    x1 = at(i)[1]
    go = grad.at[mine]
    e0[mine, :] = dot(mixt[:, 0:ROWS], go[...])
    for p, cols, rows in (
        (0, slice(0, PAIR), slice(2 * PAIR, 3 * PAIR)),
        (1, slice(0, W), slice(PAIR, 3 * PAIR)),
        (2, slice(0, W), slice(0, 2 * PAIR)),
        (3, slice(PAIR, W), slice(0, PAIR)),
    ):
        g1[mine, p * PAIR : (p + 1) * PAIR] = dot(go[:, cols], band[p, rows, :])
    dm0[...] += dot_nt(go[...], stack[0:ROWS, :])
    se, sq = esum[0], esum[1]
    for k in range(TG):
        for t in range(TILES):
            q = x1[k : k + 1, W + t * TILE : W + (t + 1) * TILE]
            r, lanes = slab_rows(k), lane_tile(t)
            res[r, lanes] = (mixed[r, lanes] + (ws * q + bb)).astype(BF16)
            e = go[r, lanes].astype(F32)
            se = se + e
            sq = sq + e * q
    esum[0] = se
    esum[1] = sq

    @pl.when(i % 4 == 3)
    def _():
        gs = gskip.at[i // 4]
        bias = jnp.concatenate([bsk[...]] * TILES, axis=1)
        z31 = stack[ROWS - C : ROWS, :]
        twos = jnp.full((16, W), 2.0, BF16)
        skip[0] = (dot(wsk[...], z31) + bias).astype(BF16)
        dsk[...] += dot_nt(jnp.concatenate([z31, twos], axis=0), gs[...])
        extra[i // 4] = dot(wskt[...], gs[...]) * (SKIP_SCALE / RES_SCALE)


def backward_kernel(
    xs, mixt, band, gl, grad, gr, z, dfil, dgat, e0, g1, esum, dsk, extra, dm0,
    pay, one, stack, dzs, acc, dmx,
):
    i = pl.program_id(0)
    mine = pl.ds(pl.multiple_of(i * ROWS, ROWS), ROWS)
    go, zb, fa, ga = (ref.at[mine] for ref in (grad, z, dfil, dgat))
    at = ((i // 4) * 6 + i % 4) * TG
    x0 = xs.at[pl.ds(pl.multiple_of(at, TG), TG)]
    x1 = xs.at[pl.ds(pl.multiple_of(at + DIL, TG), TG)]

    @pl.when(i == 0)
    def _():
        acc[...] = jnp.zeros_like(acc)
        dmx[...] = jnp.zeros_like(dmx)

    for p, halo, cols, rows in (
        (0, gl, slice(0, W), slice(0, 2 * PAIR)),
        (1, gl, slice(PAIR, W), slice(0, PAIR)),
        (2, gr, slice(0, PAIR), slice(2 * PAIR, 3 * PAIR)),
        (3, gr, slice(0, W), slice(PAIR, 3 * PAIR)),
    ):
        at = slice(p * PAIR, (p + 1) * PAIR)
        one[:, at] = (dot(halo[:, cols], band[p, rows, :]) + g1[mine, at]).astype(BF16)
    for p in range(2):
        at = slice(p * PAIR, (p + 1) * PAIR)
        stack[ROWS : 2 * ROWS, at] = dot(
            one[:, p * PAIR : (p + 3) * PAIR], band[p + 1]
        ).astype(BF16)
    stack[0:ROWS, :] = one[:, PAIR : PAIR + W]
    dzs[...] = dot(mixt[:, ROWS:], stack[...]) + e0[mine, :]
    dzs[ROWS - C : ROWS, :] += extra[i // 4] * jnp.where(i % 4 == 3, 1.0, 0.0)

    sums = [acc[j] for j in range(6)]

    def local(k, t):
        def emit():
            r, lanes = slab_rows(k), lane_tile(t)
            across = slice(W + t * TILE, W + (t + 1) * TILE)
            p, q = x0[k : k + 1, across], x1[k : k + 1, across]
            dz = dzs[r, lanes]
            df = dz * fa[r, lanes].astype(F32)
            dgt = dz * ga[r, lanes].astype(F32)
            for j, term in enumerate((df * p, df * q, df, dgt * p, dgt * q, dgt)):
                sums[j] = sums[j] + term

        return emit

    emit = spread([local(k, t) for k in range(TG) for t in range(TILES)], 2)
    for h in range(2):
        part = slice(h * ROWS, (h + 1) * ROWS)
        dmx[part, :] += dot_nt(stack[part, :], zb[...])
        emit()
    for j in range(6):
        acc[j] = sums[j]

    @pl.when(i == 7)
    def _():
        r = lax.broadcasted_iota(jnp.int32, (ROWS, ROWS), 0) // C
        c = lax.broadcasted_iota(jnp.int32, (ROWS, ROWS), 1) // C
        lane = lax.broadcasted_iota(jnp.int32, (C, TILE), 1)
        packed = jnp.zeros((C, TILE), F32)
        for h in range(3):
            m = dm0[...] if h == 0 else dmx[(h - 1) * ROWS : h * ROWS, :]
            m = jnp.where(r == c, m, 0.0)
            v = m[0:C]
            for k in range(1, TG):
                v = v + m[k * C : (k + 1) * C]
            v = v[:, :TILE] + v[:, TILE:]
            v = v + pltpu.roll(v, 64, 1)
            v = v + pltpu.roll(v, 32, 1)
            packed = jnp.where(lane // C == h, v, packed)
        packed = packed * (0.5 * RES_SCALE)
        parts = [(acc[j], 0.5 if j < 3 else 0.25) for j in range(6)] + [(esum[1], 1.0), (esum[0], 1.0)]
        for j, (a, scale) in enumerate(parts):
            s = jnp.sum(a, axis=1, keepdims=True) * (scale * RES_SCALE)
            packed = jnp.where(lane == 96 + j, s, packed)
        pay[0:C, :] = packed
        pay[C : 2 * C, :] = dsk[0:C, 0:TILE] * (0.5 * SKIP_SCALE)
        pay[2 * C : 3 * C, :] = dsk[0:C, TILE:] * (0.5 * SKIP_SCALE)
        sub = lax.broadcasted_iota(jnp.int32, (8, TILE), 0)
        pay[3 * C : PAY, :] = jnp.where(
            sub == 0, dsk[C : C + 8, 0:TILE], dsk[C : C + 8, TILE:]
        ) * (0.5 * SKIP_SCALE)


def finish_kernel(
    p0, p1, p2, p3, ws, bs, wf, wg,
    swg, dsb, dfil, dfb, dgat, dgb, dmix, dmixb, dskip, dskipb,
):
    v = (p0[...] + p1[...]) + (p2[...] + p3[...])
    wrow, brow = ws[...], bs[...]
    head = v[0:C]
    rows = head.T
    uf0, uf1, fb, ug0, ug1, gb = (head[:, 96 + j : 97 + j] for j in range(6))
    dmix[...] = head[:, 0:96]
    dfil[0] = uf0 * wrow + fb * brow
    dfil[1] = uf1 * wrow + fb * brow
    dgat[0] = ug0 * wrow + gb * brow
    dgat[1] = ug1 * wrow + gb * brow
    dfb[...] = rows[98:99]
    dgb[...] = rows[101:102]
    mb = rows[103:104]
    dmixb[...] = mb
    f0, f1, g0, g1 = wf[0].astype(F32), wf[1].astype(F32), wg[0].astype(F32), wg[1].astype(F32)
    swg[...] = (
        jnp.sum(f0 * uf0 + f1 * uf1 + g0 * ug0 + g1 * ug1, axis=0, keepdims=True)
        + rows[102:103]
    )
    dsb[...] = jnp.sum((f0 + f1) * fb + (g0 + g1) * gb, axis=0, keepdims=True) + mb
    dskip[:, 0:TILE] = v[C : 2 * C]
    dskip[:, TILE:] = v[2 * C : 3 * C]
    dskipb[:, 0:TILE] = v[3 * C : 3 * C + 1]
    dskipb[:, TILE:] = v[3 * C + 1 : 3 * C + 2]


def neighbour(value, steps):
    count = lax.axis_size("seg")
    pairs = [(i, i + steps) for i in range(max(0, -steps), min(count, count - steps))]
    return lax.ppermute(value, "seg", pairs)


def seg_ring(value, shift):
    return lax.ppermute(value, "seg", [(i, shift(i)) for i in range(lax.axis_size("seg"))])


def whole(shape):
    return pl.BlockSpec(shape, lambda *_: (0,) * len(shape))


def params(**kw):
    return pltpu.CompilerParams(vmem_limit_bytes=VMEM_LIMIT, **kw)


VMEM = pl.BlockSpec(memory_space=pltpu.VMEM)
ANY = pl.BlockSpec(memory_space=pl.ANY)
HBM = pl.BlockSpec(memory_space=pltpu.HBM)


def forward_call(xs, coef, mix, mixt, band, bandt, wsk, bsk, wskt, grad, gskip):
    rows = BR * TOUT * C
    return pl.pallas_call(
        forward_kernel,
        grid=(8,),
        out_shape=(
            jax.ShapeDtypeStruct((rows, W), BF16),
            jax.ShapeDtypeStruct((BR, SKIP, W), BF16),
            jax.ShapeDtypeStruct((rows, W), BF16),
            jax.ShapeDtypeStruct((rows, W), BF16),
            jax.ShapeDtypeStruct((rows, W), BF16),
            jax.ShapeDtypeStruct((rows, W), F32),
            jax.ShapeDtypeStruct((rows, 2 * W), F32),
            jax.ShapeDtypeStruct((2, C, TILE), F32),
            jax.ShapeDtypeStruct((C + 16, SKIP), F32),
            jax.ShapeDtypeStruct((BR, C, W), F32),
            jax.ShapeDtypeStruct((ROWS, ROWS), F32),
        ),
        in_specs=[VMEM] * 11,
        out_specs=(
            pl.BlockSpec((ROWS, W), lambda i: (i, 0)),
            pl.BlockSpec((1, SKIP, W), lambda i: (i // 4, 0, 0)),
        )
        + (VMEM,) * 9,
        scratch_shapes=[
            pltpu.VMEM((ROWS, 3 * W), BF16),
            pltpu.VMEM((ROWS, 3 * W), BF16),
            pltpu.VMEM((ROWS, 2 * W), BF16),
            pltpu.VMEM((3 * ROWS, W), BF16),
        ],
        compiler_params=params(),
        cost_estimate=pl.CostEstimate(
            flops=20_000_000_000, bytes_accessed=16_000_000, transcendentals=6_000_000
        ),
        name="forward",
    )(xs, coef, mix, mixt, band, bandt, wsk, bsk, wskt, grad, gskip)


def backward_call(xs, mixt, band, gl, go, gr, *early):
    slab = pl.BlockSpec((ROWS, W), lambda i: (i, 0))
    return pl.pallas_call(
        backward_kernel,
        grid=(8,),
        out_shape=jax.ShapeDtypeStruct((PAY, TILE), F32),
        in_specs=[VMEM] * 3 + [slab, VMEM, slab] + [VMEM] * 9,
        out_specs=VMEM,
        scratch_shapes=[
            pltpu.VMEM((ROWS, 2 * W), BF16),
            pltpu.VMEM((2 * ROWS, W), BF16),
            pltpu.VMEM((ROWS, W), F32),
            pltpu.VMEM((6, C, TILE), F32),
            pltpu.VMEM((2 * ROWS, ROWS), F32),
        ],
        compiler_params=params(),
        name="backward",
    )(xs, mixt, band, gl, go, gr, *early)


def in_hbm(a):
    return pltpu.with_memory_space_constraint(a, pltpu.HBM)


def send(speeds, cols):
    return pl.pallas_call(
        message_kernel,
        out_shape=jax.ShapeDtypeStruct((32, 4, 3 * W), BF16),
        in_specs=[HBM] * 2,
        out_specs=VMEM,
        scratch_shapes=[
            pltpu.SMEM((TILES, 3), jnp.int32),
            pltpu.VMEM((3, 16384), F32),
            pltpu.VMEM((4, 16384 + 2 * W), F32),
            pltpu.SemaphoreType.DMA((2,)),
        ],
        compiler_params=params(),
        name="message",
    )(in_hbm(cols), in_hbm(speeds))


def prepare(msg, vals, w_start, b_start, w_filter, b_filter, w_gate, b_gate, w_mix, b_mix, w_skip, b_skip):
    row = lambda a: a.reshape(1, -1)
    small = [
        row(w_start), row(b_start), w_filter, row(b_filter), w_gate, row(b_gate), w_mix, row(b_mix),
        w_skip.T, row(b_skip), *vals,
    ]
    return pl.pallas_call(
        prep_kernel,
        grid=(1,),
        out_shape=(
            jax.ShapeDtypeStruct((9 * C, TILE), F32),
            jax.ShapeDtypeStruct((ROWS, 3 * ROWS), BF16),
            jax.ShapeDtypeStruct((ROWS, 3 * ROWS), BF16),
            jax.ShapeDtypeStruct((SKIP, C), BF16),
            jax.ShapeDtypeStruct((SKIP, TILE), F32),
            jax.ShapeDtypeStruct((4, 3 * PAIR, PAIR), BF16),
            jax.ShapeDtypeStruct((4, 3 * PAIR, PAIR), BF16),
            jax.ShapeDtypeStruct((BR * T_IN, 3 * W), F32),
        ),
        in_specs=[whole(a.shape) for a in small] + [VMEM],
        out_specs=(VMEM,) * 8,
        compiler_params=params(),
        name="prep",
    )(*(in_hbm(a) for a in small), msg)


def body(
    speeds, w_start, b_start, w_filter, b_filter, w_gate, b_gate, adj_cols, adj_vals,
    w_mix, b_mix, w_skip, b_skip, grad_res, grad_skip,
):
    barrier = lax.optimization_barrier
    grad = grad_res.reshape(BR * TOUT * C, W)
    msg = send(speeds, adj_cols)
    msg, vals = barrier((msg, adj_vals))
    msg = lax.all_to_all(msg, "seg", split_axis=0, concat_axis=0, tiled=True)
    vals = (neighbour(vals, 1), adj_vals, neighbour(vals, -1))
    *vals, grad_now = barrier((*vals, grad))
    grad_l, grad_r = neighbour(grad_now, 1), neighbour(grad_now, -1)
    coef, mix, mixt, wsk, bsk, band, bandt, xs = prepare(
        msg, vals, w_start, b_start, w_filter, b_filter, w_gate, b_gate, w_mix, b_mix, w_skip, b_skip
    )
    res, skip, *early = forward_call(
        xs, coef, mix, mixt, band, bandt, wsk, bsk, w_skip.T, grad, grad_skip
    )
    v = backward_call(xs, mixt, band, grad_l, grad, grad_r, *early)

    v = v + seg_ring(v, lambda i: i ^ 1)
    v = v + sum(seg_ring(v, lambda i, k=k: (i // 8) * 8 + ((i // 2 + k) % 4) * 2 + i % 2) for k in (1, 2, 3))
    v = v + sum(seg_ring(v, lambda i, k=k: (i + 8 * k) % 32) for k in (1, 2, 3))
    others = [lax.ppermute(v, "rep", [(i, (i + k) % 4) for i in range(4)]) for k in (1, 2, 3)]

    row = jax.ShapeDtypeStruct((1, C), F32)
    taps = jax.ShapeDtypeStruct((2, C, C), F32)
    small = (v, *others, w_start.reshape(1, C), b_start.reshape(1, C), w_filter, w_gate)
    swg, dsb, dfil, dfb, dgat, dgb, dmix, dmixb, dskip, dskipb = pl.pallas_call(
        finish_kernel,
        grid=(1,),
        out_shape=(
            row, row, taps, row, taps, row, jax.ShapeDtypeStruct((C, 3 * C), F32), row,
            jax.ShapeDtypeStruct((C, SKIP), F32), jax.ShapeDtypeStruct((1, SKIP), F32),
        ),
        in_specs=[whole(a.shape) for a in small],
        out_specs=(whole((1, C)), whole((1, C)), whole((2, C, C)), whole((1, C)), whole((2, C, C)),
                   whole((1, C)), whole((C, 3 * C)), whole((1, C)), whole((C, SKIP)), whole((1, SKIP))),
        compiler_params=params(),
        name="finish",
    )(*small)
    vec = lambda a: a.reshape(-1)
    return (
        res.reshape(BR, TOUT, C, W), skip, vec(swg), vec(dsb), dfil, vec(dfb), dgat, vec(dgb),
        dmix, vec(dmixb), dskip.T, vec(dskipb),
    )


def solution(mesh):
    placed = (
        P(("rep", "seg"), None), P(), P(), P(), P(), P(), P(), P("seg", None),
        P("seg", None, None, None), P(), P(), P(), P(), P("rep", None, None, "seg"),
        P("rep", None, "seg"),
    )
    return jax.shard_map(
        body,
        mesh=mesh,
        in_specs=placed,
        out_specs=(P("rep", None, None, "seg"), P("rep", None, "seg")) + (P(),) * 10,
        check_vma=False,
    )
```

```python
import functools
import math

import jax
import jax.numpy as jnp
from jax import lax
from jax.experimental import pallas as pl
from jax.experimental.pallas import tpu as pltpu
from jax.sharding import PartitionSpec as P

C = 32
SKIP = 256
TILE = 128
DIL = 16
TOUT = 32
T_IN = 48
BR = 2
TILES = 4
W = TILES * TILE
PAIR = 2 * TILE
TG = 8
ROWS = TG * C
F32 = jnp.float32
BF16 = jnp.bfloat16
A0F, A1F, CF, A0G, A1G, CG, WS, BS, BM = range(9)
PAY = 104
RES_SCALE = 1.0 / math.sqrt(8 * TOUT * 16384)
SKIP_SCALE = 1.0 / math.sqrt(8 * 16384)
VMEM_LIMIT = 20 * 1024 * 1024


def dot(a, b):
    return jnp.dot(a, b, preferred_element_type=F32)


def dot_nt(a, b):
    return lax.dot_general(a, b, (((1,), (1,)), ((), ())), preferred_element_type=F32)


def column(row):
    n = row.shape[1]
    r = lax.broadcasted_iota(jnp.int32, (n, n), 0)
    c = lax.broadcasted_iota(jnp.int32, (n, n), 1)
    return jnp.sum(jnp.where(r == c, jnp.broadcast_to(row, (n, n)), 0.0), axis=1, keepdims=True)


def block_diag(w):
    row = jnp.concatenate([w] * TG, axis=1)
    full = jnp.concatenate([row] * TG, axis=0)
    r = lax.broadcasted_iota(jnp.int32, (ROWS, ROWS), 0) // C
    c = lax.broadcasted_iota(jnp.int32, (ROWS, ROWS), 1) // C
    return jnp.where(r == c, full, 0.0)


def message_kernel(cols_hbm, speeds, msg, cols, rows, wide, sems):
    loads = [
        pltpu.make_async_copy(speeds, rows, sems.at[0]),
        pltpu.make_async_copy(cols_hbm, cols, sems.at[1]),
    ]
    for copy in loads:
        copy.start()
    wide[:, 0:W] = jnp.zeros((4, W), F32)
    wide[:, W + 16384 :] = jnp.zeros((4, W), F32)
    loads[0].wait()
    loads[1].wait()
    wide[0:3, W : W + 16384] = rows[...]
    base = lax.axis_index("seg") * TILES
    offsets = jnp.concatenate(
        [
            jnp.broadcast_to((cols[t, k] - (base + t)).astype(F32), (4, TILE))
            for t in range(TILES)
            for k in range(3)
        ],
        axis=1,
    )
    row = lax.broadcasted_iota(jnp.int32, (4, 3 * W), 0)
    for d in range(32):
        msg[d] = jnp.where(row == 3, offsets, wide[:, d * W : (d + 3) * W]).astype(BF16)


def prep_kernel(
    ws, bs, wf, bf, wg, bg, wm, bm, wskt, bsk, vl, vo, vr, msg,
    coef, mix, mixt, wsk, bskc, band, bandt, xs,
):
    wrow, brow = ws[...], bs[...]

    def put(i, col):
        coef[i * C : (i + 1) * C, :] = jnp.broadcast_to(col, (C, TILE))

    def lane_sum(m):
        return jnp.sum(m, axis=1, keepdims=True)

    for w, bias, base, scale in ((wf, bf, A0F, 1.0), (wg, bg, A0G, 0.5)):
        w0, w1 = w[0].astype(F32), w[1].astype(F32)
        put(base, lane_sum(w0 * wrow) * scale)
        put(base + 1, lane_sum(w1 * wrow) * scale)
        put(base + 2, (lane_sum((w0 + w1) * brow) + column(bias[...])) * scale)
    put(WS, column(wrow))
    put(BS, column(brow))
    put(BM, column(bm[...]))
    for h in range(3):
        w = wm[:, h * C : (h + 1) * C].astype(F32)
        mix[:, h * ROWS : (h + 1) * ROWS] = block_diag(w * 0.5).astype(BF16)
        mixt[:, h * ROWS : (h + 1) * ROWS] = block_diag(w.T).astype(BF16)
    wsk[...] = (wskt[...].astype(F32) * 0.5).T.astype(BF16)
    bskc[...] = jnp.broadcast_to(column(bsk[...]), (SKIP, TILE))

    for i in range(32):
        xs[3 * i : 3 * i + 3, :] = msg[i].astype(F32)[0:3]

    def store(dst, row, col, v):
        j = col // 2 - 1
        at = row - 2 * j
        if 0 <= j < 4 and 0 <= at < 6:
            dst[j, at * TILE : (at + 1) * TILE, (col % 2) * TILE : (col % 2 + 1) * TILE] = v

    zero = jnp.zeros((TILE, TILE), BF16)
    for dst in (band, bandt):
        for j in range(4):
            dst[j, 0:TILE, TILE:] = zero
            dst[j, 5 * TILE :, 0:TILE] = zero
    seg = lax.axis_index("seg")
    for src, vals in enumerate((vl, vo, vr)):
        sender = jnp.clip(seg + src - 1, 0, 31)
        for t in range(TILES):
            m = src * TILES + t
            v0, v1, v2 = (vals[t, k] for k in range(3))
            u0, u1, u2 = v0.T, v1.T, v2.T

            def off(k, t=t, sender=sender):
                return msg[sender, :, (t * 3 + k) * TILE : (t * 3 + k + 1) * TILE].astype(F32)[3:4]

            o1, o2 = off(1), off(2)
            store(band, m, m, v0)
            store(bandt, m, m, u0)
            for o in (-2, -1, 1, 2):
                q = m + o
                if not 0 <= q < 12:
                    continue
                c2 = jnp.broadcast_to(jnp.where(o2 == o, 1.0, 0.0).astype(BF16), (TILE, TILE))
                v, u = c2 * v2, c2 * u2
                if abs(o) == 2:
                    c1 = jnp.broadcast_to(jnp.where(o1 == o, 1.0, 0.0).astype(BF16), (TILE, TILE))
                    v, u = v + c1 * v1, u + c1 * u1
                store(band, m, q, v)
                store(bandt, q, m, u)


def hops(ext, one, band, put, between):
    for p in range(4):
        one[:, p * PAIR : (p + 1) * PAIR] = dot(
            ext[:, p * PAIR : (p + 3) * PAIR], band[p]
        ).astype(BF16)
        between()
    for p in range(2):
        put(p, dot(one[:, p * PAIR : (p + 3) * PAIR], band[p + 1]).astype(BF16))
        between()


def coefs(coef, *which):
    return [coef[i * C : (i + 1) * C, :] for i in which]


def spread(bodies, slots):
    queue = list(bodies)
    share = -(-len(queue) // slots)

    def emit():
        for _ in range(min(share, len(queue))):
            queue.pop(0)()

    return emit


def lane_tile(t):
    return slice(t * TILE, (t + 1) * TILE)


def slab_rows(k):
    return slice(k * C, (k + 1) * C)


def gates(coef, p, q):
    a0f, a1f, cf, a0g, a1g, cg = coefs(coef, A0F, A1F, CF, A0G, A1G, CG)
    return jnp.tanh(a0f * p + a1f * q + cf), jnp.tanh(a0g * p + a1g * q + cg) + 1.0


def forward_kernel(
    xs, coef, mix, mixt, band, bandt, wsk, bsk, wskt, grad, gskip,
    res, skip, z, dfil, dgat, e0, g1, esum, dsk, extra, dm0, ahead, zext, one, stack,
):
    i = pl.program_id(0)

    def at(step):
        row = ((step // 4) * 6 + step % 4) * TG
        return (
            xs.at[pl.ds(pl.multiple_of(row, TG), TG)],
            xs.at[pl.ds(pl.multiple_of(row + DIL, TG), TG)],
        )

    def look_ahead(step, k, t):
        x0, x1 = at(step)

        def emit():
            lanes = lane_tile(t)
            f, u = gates(coef, x0[k : k + 1, lanes], x1[k : k + 1, lanes])
            fu = f * u
            ahead[slab_rows(k), lanes] = fu.astype(BF16)
            if 4 <= t < 8:
                rows = pl.ds(pl.multiple_of(step * ROWS + k * C, C), C)
                dfil[rows, lane_tile(t - 4)] = (u - f * fu).astype(BF16)
                dgat[rows, lane_tile(t - 4)] = (fu * (2.0 - u)).astype(BF16)

        return emit

    @pl.when(i == 0)
    def _():
        esum[...] = jnp.zeros_like(esum)
        dsk[...] = jnp.zeros_like(dsk)
        dm0[...] = jnp.zeros_like(dm0)
        for k in range(TG):
            for t in range(12):
                look_ahead(i, k, t)()

    mine = pl.ds(pl.multiple_of(i * ROWS, ROWS), ROWS)
    zext[...] = ahead[...]
    stack[0:ROWS, :] = ahead[:, W : 2 * W]
    z[mine, :] = ahead[:, W : 2 * W]
    ahead_step = jnp.minimum(i + 1, 7)
    emit = spread([look_ahead(ahead_step, k, t) for k in range(TG) for t in range(12)], 6)

    def put(p, v):
        stack[2 * ROWS : 3 * ROWS, p * PAIR : (p + 1) * PAIR] = v

    hops(zext, one, bandt, put, emit)
    stack[ROWS : 2 * ROWS, :] = one[:, PAIR : PAIR + W]
    mixed = dot(mix[...], stack[...])
    ws, bs, bm = coefs(coef, WS, BS, BM)
    bb = bs + bm
    x1 = at(i)[1]
    go = grad.at[mine]
    e0[mine, :] = dot(mixt[:, 0:ROWS], go[...])
    for p, cols, rows in (
        (0, slice(0, PAIR), slice(2 * PAIR, 3 * PAIR)),
        (1, slice(0, W), slice(PAIR, 3 * PAIR)),
        (2, slice(0, W), slice(0, 2 * PAIR)),
        (3, slice(PAIR, W), slice(0, PAIR)),
    ):
        g1[mine, p * PAIR : (p + 1) * PAIR] = dot(go[:, cols], band[p, rows, :])
    dm0[...] += dot_nt(go[...], stack[0:ROWS, :])
    se, sq = esum[0], esum[1]
    for k in range(TG):
        for t in range(TILES):
            q = x1[k : k + 1, W + t * TILE : W + (t + 1) * TILE]
            r, lanes = slab_rows(k), lane_tile(t)
            res[r, lanes] = (mixed[r, lanes] + (ws * q + bb)).astype(BF16)
            e = go[r, lanes].astype(F32)
            se = se + e
            sq = sq + e * q
    esum[0] = se
    esum[1] = sq

    @pl.when(i % 4 == 3)
    def _():
        gs = gskip.at[i // 4]
        bias = jnp.concatenate([bsk[...]] * TILES, axis=1)
        z31 = stack[ROWS - C : ROWS, :]
        twos = jnp.full((16, W), 2.0, BF16)
        skip[0] = (dot(wsk[...], z31) + bias).astype(BF16)
        dsk[...] += dot_nt(jnp.concatenate([z31, twos], axis=0), gs[...])
        extra[i // 4] = dot(wskt[...], gs[...]) * (SKIP_SCALE / RES_SCALE)


def backward_kernel(
    xs, mixt, band, gl, grad, gr, z, dfil, dgat, e0, g1, esum, dsk, extra, dm0,
    pay, one, stack, dzs, acc, dmx,
):
    i = pl.program_id(0)
    mine = pl.ds(pl.multiple_of(i * ROWS, ROWS), ROWS)
    go, zb, fa, ga = (ref.at[mine] for ref in (grad, z, dfil, dgat))
    at = ((i // 4) * 6 + i % 4) * TG
    x0 = xs.at[pl.ds(pl.multiple_of(at, TG), TG)]
    x1 = xs.at[pl.ds(pl.multiple_of(at + DIL, TG), TG)]

    @pl.when(i == 0)
    def _():
        acc[...] = jnp.zeros_like(acc)
        dmx[...] = jnp.zeros_like(dmx)

    for p, halo, cols, rows in (
        (0, gl, slice(0, W), slice(0, 2 * PAIR)),
        (1, gl, slice(PAIR, W), slice(0, PAIR)),
        (2, gr, slice(0, PAIR), slice(2 * PAIR, 3 * PAIR)),
        (3, gr, slice(0, W), slice(PAIR, 3 * PAIR)),
    ):
        at = slice(p * PAIR, (p + 1) * PAIR)
        one[:, at] = (dot(halo[:, cols], band[p, rows, :]) + g1[mine, at]).astype(BF16)
    for p in range(2):
        at = slice(p * PAIR, (p + 1) * PAIR)
        stack[ROWS : 2 * ROWS, at] = dot(
            one[:, p * PAIR : (p + 3) * PAIR], band[p + 1]
        ).astype(BF16)
    stack[0:ROWS, :] = one[:, PAIR : PAIR + W]
    dzs[...] = dot(mixt[:, ROWS:], stack[...]) + e0[mine, :]
    dzs[ROWS - C : ROWS, :] += extra[i // 4] * jnp.where(i % 4 == 3, 1.0, 0.0)

    sums = [acc[j] for j in range(6)]

    def local(k, t):
        def emit():
            r, lanes = slab_rows(k), lane_tile(t)
            across = slice(W + t * TILE, W + (t + 1) * TILE)
            p, q = x0[k : k + 1, across], x1[k : k + 1, across]
            dz = dzs[r, lanes]
            df = dz * fa[r, lanes].astype(F32)
            dgt = dz * ga[r, lanes].astype(F32)
            for j, term in enumerate((df * p, df * q, df, dgt * p, dgt * q, dgt)):
                sums[j] = sums[j] + term

        return emit

    emit = spread([local(k, t) for k in range(TG) for t in range(TILES)], 2)
    for h in range(2):
        part = slice(h * ROWS, (h + 1) * ROWS)
        dmx[part, :] += dot_nt(stack[part, :], zb[...])
        emit()
    for j in range(6):
        acc[j] = sums[j]

    @pl.when(i == 7)
    def _():
        r = lax.broadcasted_iota(jnp.int32, (ROWS, ROWS), 0) // C
        c = lax.broadcasted_iota(jnp.int32, (ROWS, ROWS), 1) // C
        lane = lax.broadcasted_iota(jnp.int32, (C, TILE), 1)
        packed = jnp.zeros((C, TILE), F32)
        for h in range(3):
            m = dm0[...] if h == 0 else dmx[(h - 1) * ROWS : h * ROWS, :]
            m = jnp.where(r == c, m, 0.0)
            v = m[0:C]
            for k in range(1, TG):
                v = v + m[k * C : (k + 1) * C]
            v = v[:, :TILE] + v[:, TILE:]
            v = v + pltpu.roll(v, 64, 1)
            v = v + pltpu.roll(v, 32, 1)
            packed = jnp.where(lane // C == h, v, packed)
        packed = packed * (0.5 * RES_SCALE)
        parts = [(acc[j], 0.5 if j < 3 else 0.25) for j in range(6)] + [(esum[1], 1.0), (esum[0], 1.0)]
        for j, (a, scale) in enumerate(parts):
            s = jnp.sum(a, axis=1, keepdims=True) * (scale * RES_SCALE)
            packed = jnp.where(lane == 96 + j, s, packed)
        pay[0:C, :] = packed
        pay[C : 2 * C, :] = dsk[0:C, 0:TILE] * (0.5 * SKIP_SCALE)
        pay[2 * C : 3 * C, :] = dsk[0:C, TILE:] * (0.5 * SKIP_SCALE)
        sub = lax.broadcasted_iota(jnp.int32, (8, TILE), 0)
        pay[3 * C : PAY, :] = jnp.where(
            sub == 0, dsk[C : C + 8, 0:TILE], dsk[C : C + 8, TILE:]
        ) * (0.5 * SKIP_SCALE)


def finish_kernel(
    p0, p1, p2, p3, ws, bs, wf, wg,
    swg, dsb, dfil, dfb, dgat, dgb, dmix, dmixb, dskip, dskipb,
):
    v = (p0[...] + p1[...]) + (p2[...] + p3[...])
    wrow, brow = ws[...], bs[...]
    head = v[0:C]
    rows = head.T
    uf0, uf1, fb, ug0, ug1, gb = (head[:, 96 + j : 97 + j] for j in range(6))
    dmix[...] = head[:, 0:96]
    dfil[0] = uf0 * wrow + fb * brow
    dfil[1] = uf1 * wrow + fb * brow
    dgat[0] = ug0 * wrow + gb * brow
    dgat[1] = ug1 * wrow + gb * brow
    dfb[...] = rows[98:99]
    dgb[...] = rows[101:102]
    mb = rows[103:104]
    dmixb[...] = mb
    f0, f1, g0, g1 = wf[0].astype(F32), wf[1].astype(F32), wg[0].astype(F32), wg[1].astype(F32)
    swg[...] = (
        jnp.sum(f0 * uf0 + f1 * uf1 + g0 * ug0 + g1 * ug1, axis=0, keepdims=True)
        + rows[102:103]
    )
    dsb[...] = jnp.sum((f0 + f1) * fb + (g0 + g1) * gb, axis=0, keepdims=True) + mb
    dskip[:, 0:TILE] = v[C : 2 * C]
    dskip[:, TILE:] = v[2 * C : 3 * C]
    dskipb[:, 0:TILE] = v[3 * C : 3 * C + 1]
    dskipb[:, TILE:] = v[3 * C + 1 : 3 * C + 2]


def neighbour(value, steps):
    count = lax.axis_size("seg")
    pairs = [(i, i + steps) for i in range(max(0, -steps), min(count, count - steps))]
    return lax.ppermute(value, "seg", pairs)


def seg_ring(value, shift):
    return lax.ppermute(value, "seg", [(i, shift(i)) for i in range(lax.axis_size("seg"))])


def whole(shape):
    return pl.BlockSpec(shape, lambda *_: (0,) * len(shape))


def params(**kw):
    return pltpu.CompilerParams(vmem_limit_bytes=VMEM_LIMIT, **kw)


VMEM = pl.BlockSpec(memory_space=pltpu.VMEM)
ANY = pl.BlockSpec(memory_space=pl.ANY)
HBM = pl.BlockSpec(memory_space=pltpu.HBM)


def forward_call(xs, coef, mix, mixt, band, bandt, wsk, bsk, wskt, grad, gskip):
    rows = BR * TOUT * C
    return pl.pallas_call(
        forward_kernel,
        grid=(8,),
        out_shape=(
            jax.ShapeDtypeStruct((rows, W), BF16),
            jax.ShapeDtypeStruct((BR, SKIP, W), BF16),
            jax.ShapeDtypeStruct((rows, W), BF16),
            jax.ShapeDtypeStruct((rows, W), BF16),
            jax.ShapeDtypeStruct((rows, W), BF16),
            jax.ShapeDtypeStruct((rows, W), F32),
            jax.ShapeDtypeStruct((rows, 2 * W), F32),
            jax.ShapeDtypeStruct((2, C, TILE), F32),
            jax.ShapeDtypeStruct((C + 16, SKIP), F32),
            jax.ShapeDtypeStruct((BR, C, W), F32),
            jax.ShapeDtypeStruct((ROWS, ROWS), F32),
        ),
        in_specs=[VMEM] * 11,
        out_specs=(
            pl.BlockSpec((ROWS, W), lambda i: (i, 0)),
            pl.BlockSpec((1, SKIP, W), lambda i: (i // 4, 0, 0)),
        )
        + (VMEM,) * 9,
        scratch_shapes=[
            pltpu.VMEM((ROWS, 3 * W), BF16),
            pltpu.VMEM((ROWS, 3 * W), BF16),
            pltpu.VMEM((ROWS, 2 * W), BF16),
            pltpu.VMEM((3 * ROWS, W), BF16),
        ],
        compiler_params=params(),
        cost_estimate=pl.CostEstimate(
            flops=20_000_000_000, bytes_accessed=16_000_000, transcendentals=6_000_000
        ),
        name="forward",
    )(xs, coef, mix, mixt, band, bandt, wsk, bsk, wskt, grad, gskip)


def backward_call(xs, mixt, band, gl, go, gr, *early):
    slab = pl.BlockSpec((ROWS, W), lambda i: (i, 0))
    return pl.pallas_call(
        backward_kernel,
        grid=(8,),
        out_shape=jax.ShapeDtypeStruct((PAY, TILE), F32),
        in_specs=[VMEM] * 3 + [slab, VMEM, slab] + [VMEM] * 9,
        out_specs=VMEM,
        scratch_shapes=[
            pltpu.VMEM((ROWS, 2 * W), BF16),
            pltpu.VMEM((2 * ROWS, W), BF16),
            pltpu.VMEM((ROWS, W), F32),
            pltpu.VMEM((6, C, TILE), F32),
            pltpu.VMEM((2 * ROWS, ROWS), F32),
        ],
        compiler_params=params(),
        name="backward",
    )(xs, mixt, band, gl, go, gr, *early)


def in_hbm(a):
    return pltpu.with_memory_space_constraint(a, pltpu.HBM)


def send(speeds, cols):
    return pl.pallas_call(
        message_kernel,
        out_shape=jax.ShapeDtypeStruct((32, 4, 3 * W), BF16),
        in_specs=[HBM] * 2,
        out_specs=VMEM,
        scratch_shapes=[
            pltpu.SMEM((TILES, 3), jnp.int32),
            pltpu.VMEM((3, 16384), F32),
            pltpu.VMEM((4, 16384 + 2 * W), F32),
            pltpu.SemaphoreType.DMA((2,)),
        ],
        compiler_params=params(),
        name="message",
    )(in_hbm(cols), in_hbm(speeds))


def prepare(msg, vals, w_start, b_start, w_filter, b_filter, w_gate, b_gate, w_mix, b_mix, w_skip, b_skip):
    row = lambda a: a.reshape(1, -1)
    small = [
        row(w_start), row(b_start), w_filter, row(b_filter), w_gate, row(b_gate), w_mix, row(b_mix),
        w_skip.T, row(b_skip), *vals,
    ]
    return pl.pallas_call(
        prep_kernel,
        grid=(1,),
        out_shape=(
            jax.ShapeDtypeStruct((9 * C, TILE), F32),
            jax.ShapeDtypeStruct((ROWS, 3 * ROWS), BF16),
            jax.ShapeDtypeStruct((ROWS, 3 * ROWS), BF16),
            jax.ShapeDtypeStruct((SKIP, C), BF16),
            jax.ShapeDtypeStruct((SKIP, TILE), F32),
            jax.ShapeDtypeStruct((4, 3 * PAIR, PAIR), BF16),
            jax.ShapeDtypeStruct((4, 3 * PAIR, PAIR), BF16),
            jax.ShapeDtypeStruct((BR * T_IN, 3 * W), F32),
        ),
        in_specs=[whole(a.shape) for a in small] + [VMEM],
        out_specs=(VMEM,) * 8,
        compiler_params=params(),
        name="prep",
    )(*(in_hbm(a) for a in small), msg)


def body(
    speeds, w_start, b_start, w_filter, b_filter, w_gate, b_gate, adj_cols, adj_vals,
    w_mix, b_mix, w_skip, b_skip, grad_res, grad_skip,
):
    barrier = lax.optimization_barrier
    grad = grad_res.reshape(BR * TOUT * C, W)
    msg = send(speeds, adj_cols)
    msg, vals = barrier((msg, adj_vals))
    msg = lax.all_to_all(msg, "seg", split_axis=0, concat_axis=0, tiled=True)
    vals = (neighbour(vals, 1), adj_vals, neighbour(vals, -1))
    *vals, grad_now = barrier((*vals, grad))
    grad_l, grad_r = neighbour(grad_now, 1), neighbour(grad_now, -1)
    coef, mix, mixt, wsk, bsk, band, bandt, xs = prepare(
        msg, vals, w_start, b_start, w_filter, b_filter, w_gate, b_gate, w_mix, b_mix, w_skip, b_skip
    )
    res, skip, *early = forward_call(
        xs, coef, mix, mixt, band, bandt, wsk, bsk, w_skip.T, grad, grad_skip
    )
    v = backward_call(xs, mixt, band, grad_l, grad, grad_r, *early)

    v = v + seg_ring(v, lambda i: i ^ 1)
    v = v + sum(seg_ring(v, lambda i, k=k: (i // 8) * 8 + ((i // 2 + k) % 4) * 2 + i % 2) for k in (1, 3, 2))
    v = v + sum(seg_ring(v, lambda i, k=k: (i + 8 * k) % 32) for k in (1, 3, 2))
    others = [lax.ppermute(v, "rep", [(i, (i + k) % 4) for i in range(4)]) for k in (1, 3, 2)]

    row = jax.ShapeDtypeStruct((1, C), F32)
    taps = jax.ShapeDtypeStruct((2, C, C), F32)
    small = (v, *others, w_start.reshape(1, C), b_start.reshape(1, C), w_filter, w_gate)
    swg, dsb, dfil, dfb, dgat, dgb, dmix, dmixb, dskip, dskipb = pl.pallas_call(
        finish_kernel,
        grid=(1,),
        out_shape=(
            row, row, taps, row, taps, row, jax.ShapeDtypeStruct((C, 3 * C), F32), row,
            jax.ShapeDtypeStruct((C, SKIP), F32), jax.ShapeDtypeStruct((1, SKIP), F32),
        ),
        in_specs=[whole(a.shape) for a in small],
        out_specs=(whole((1, C)), whole((1, C)), whole((2, C, C)), whole((1, C)), whole((2, C, C)),
                   whole((1, C)), whole((C, 3 * C)), whole((1, C)), whole((C, SKIP)), whole((1, SKIP))),
        compiler_params=params(),
        name="finish",
    )(*small)
    vec = lambda a: a.reshape(-1)
    return (
        res.reshape(BR, TOUT, C, W), skip, vec(swg), vec(dsb), dfil, vec(dfb), dgat, vec(dgb),
        dmix, vec(dmixb), dskip.T, vec(dskipb),
    )


def solution(mesh):
    placed = (
        P(("rep", "seg"), None), P(), P(), P(), P(), P(), P(), P("seg", None),
        P("seg", None, None, None), P(), P(), P(), P(), P("rep", None, None, "seg"),
        P("rep", None, "seg"),
    )
    return jax.shard_map(
        body,
        mesh=mesh,
        in_specs=placed,
        out_specs=(P("rep", None, None, "seg"), P("rep", None, "seg")) + (P(),) * 10,
        check_vma=False,
    )
```
